256 devices in a mesh: ex: 16 (over z, y_lo), par: 16 (over y_hi, x, core).
Axes of the slice: x: 4, y: 4 (y_hi: 2, y_lo: 2; y = y_hi * 2 + y_lo), z: 8, core: 2. Of those that a mesh axis runs over, the one named last changes fastest.
Arguments:
- gradients: bfloat16 [1024, 65536], P('ex', 'par'), may hold values from -6 to 6
- inverse_gram: bfloat16 [16384, 16384], P('par', 'ex'), may hold values from -1 to 3
- hash_words: int32 [4], replicated, may hold values from 1 to 2147483646
Outputs:
- scores: float32 [1024, 1024], P('par', 'ex')
The draws below stay inside these ranges and needn't reach their ends.
All inputs are finite; a program needn't handle non-finite values.
Results may differ from the reference program's by a relative error of at most 0.0003.
Values may be sent and summed in bfloat16 or wider, within the bound.
No kernel may reach another device: no remote copies, remote signals or barrier semaphores. Data moves between devices by JAX's collectives and lax.ppermute only.
A program may use at most 64 MiB of HBM per device.

```python
import math
import jax
import jax.numpy as jnp
from jax import lax

FEATURES = 16384
EXAMPLES = 1024
PARAMS = 65536


def draw_inverse_gram(key, part):
    off_key, diag_key = jax.random.split(jax.random.fold_in(key, 11))
    spread = 0.5 / math.sqrt(FEATURES)
    off_part = jax.random.truncated_normal(off_key, -4.0, 4.0, (FEATURES, FEATURES), jnp.float32) * spread
    diagonal = jax.random.uniform(diag_key, (FEATURES,), jnp.float32, 0.5, 2.0)
    diag_ids = jnp.arange(FEATURES)
    return off_part.at[diag_ids, diag_ids].add(diagonal).astype(jnp.bfloat16)


def touch_ends(array, key, smallest, high):
    index_at = [jax.random.randint(jax.random.fold_in(key, axis), (), 0, length) for axis, length in enumerate(array.shape)]
    longest = array.shape.index(max(array.shape))
    next_to = index_at[:longest] + [(index_at[longest] + 1) % array.shape[longest]] + index_at[longest + 1:]
    return array.at[tuple(index_at)].set(smallest).at[tuple(next_to)].set(high)


def shard_levels(own_key, shape, pieces, low, largest):
    loudness = 1.0
    for dim, parts in pieces:
        draws = jax.random.uniform(jax.random.fold_in(jax.random.fold_in(own_key, 6), dim), (parts,), jnp.float32, low / len(pieces), largest / len(pieces))
        loudness = loudness * jnp.repeat(jnp.exp(draws), shape[dim] // parts).reshape((-1,) + (1,) * (len(shape) - 1 - dim))
    return loudness


def scatter_about(own_key, shape, deviation, most, cuts=(), held_as=jnp.bfloat16):
    entries = deviation * jax.random.normal(own_key, shape, jnp.float32)
    if cuts:
        entries = entries * shard_levels(own_key, shape, cuts, -0.22, 0.18)
    return jnp.clip(entries, -most, most).astype(held_as)


def setup_inputs(seed: int = 0) -> dict:
    key_list = jax.random.split(jax.random.key(seed), 4)
    gradients = scatter_about(key_list[0], (EXAMPLES, PARAMS), 1.0, 6.0, ((0, 16), (1, 16)))
    inverse_gram = draw_inverse_gram(jax.random.fold_in(key_list[3], 71), 0)
    hash_words = touch_ends(jax.random.randint(key_list[2], (4,), 1, 2147483647), jax.random.fold_in(key_list[2], 1), 1, 2147483646).astype(jnp.int32)
    return {"gradients": gradients, "inverse_gram": inverse_gram, "hash_words": hash_words}


def shifted(values, amount):
    return lax.shift_right_logical(values, jnp.full(values.shape, amount, jnp.int32))


def hash_table(hash_words, row_start, row_count, col_start, col_count):
    row_ids = lax.broadcasted_iota(jnp.int32, (row_count, col_count), 0) + row_start
    col_ids = lax.broadcasted_iota(jnp.int32, (row_count, col_count), 1) + col_start
    mixed = row_ids * FEATURES + col_ids
    mixed = mixed * (hash_words[0] | 1) + hash_words[1]
    mixed = mixed ^ shifted(mixed, 15)
    mixed = mixed * (hash_words[2] | 1)
    mixed = mixed ^ shifted(mixed, 13)
    mixed = mixed * (hash_words[3] | 1)
    mixed = mixed ^ shifted(mixed, 16)
    top_bit = shifted(mixed, 31)
    return ((1 - 2 * top_bit).astype(jnp.float32) * (FEATURES ** -0.5)).astype(jnp.bfloat16)


def reference(gradients, inverse_gram, hash_words):
    param_count = gradients.shape[1]
    col_width = min(1024, FEATURES)
    block_count = FEATURES // col_width

    def column_block(col_start):
        sign_table = hash_table(hash_words, 0, param_count, col_start, col_width)
        return jnp.dot(gradients, sign_table, preferred_element_type=jnp.float32)

    col_starts = jnp.arange(block_count, dtype=jnp.int32) * col_width
    blocks = lax.map(column_block, col_starts)
    features = jnp.transpose(blocks, (1, 0, 2)).reshape(gradients.shape[0], FEATURES).astype(jnp.bfloat16)
    conditioned = jnp.dot(features, inverse_gram, preferred_element_type=jnp.float32).astype(jnp.bfloat16)
    pairs = jnp.dot(conditioned, features.T, preferred_element_type=jnp.float32)
    return pairs * (FEATURES ** -0.5)
```

```python
import jax
import jax.numpy as jnp
from jax import lax
from jax.experimental import pallas as pl
from jax.experimental.pallas import tpu as pltpu
from jax.sharding import Mesh
from jax.sharding import PartitionSpec as P

FEATURES = 16384
SCALE = FEATURES ** (-0.5)
BF16 = jnp.bfloat16
F32 = jnp.float32

EX = ("zh", "zl", "yl")
CHIPS = ("yh", "x")
PAR = ("yh", "x", "c")


def shifted(values, amount):
    return lax.shift_right_logical(values, jnp.full(values.shape, amount, jnp.int32))


def signs(hash_words, row_start, rows, cols):
    m0 = hash_words[0] | 1
    row_ids = lax.broadcasted_iota(jnp.int32, (rows, cols.shape[1]), 0)
    mixed = row_ids * (FEATURES * m0) + (cols * m0 + (row_start * (FEATURES * m0) + hash_words[1]))
    mixed = mixed ^ shifted(mixed, 15)
    mixed = mixed * (hash_words[2] | 1)
    mixed = mixed ^ shifted(mixed, 13)
    mixed = mixed * (hash_words[3] | 1)
    return jnp.where(mixed < 0, BF16(-1), BF16(1))


def project_kernel(words, mine, next_y, next_z, diag_a, diag_b, *rest):
    other = rest[:5]
    out, examples, total = rest[5:]
    step = pl.program_id(0)
    half = pl.num_programs(0) // 2
    me = lax.axis_index("zl") * 2 + lax.axis_index("yl")
    core = lax.axis_index("c")
    chip = lax.axis_index("yh") * 4 + lax.axis_index("x")
    slice_id = lax.axis_index("yl") * 4 + lax.axis_index("zl") * 2 + core
    rows, depth = mine.shape

    def fill(own, y, z, da, db):
        def at(flip, offset=0):
            return pl.multiple_of((me ^ flip) * rows + offset, 32)

        examples[pl.ds(at(0), rows), :] = own[...]
        examples[pl.ds(at(1), rows), :] = y[...]
        examples[pl.ds(at(2), rows), :] = z[...]
        examples[pl.ds(at(3), rows // 2), :] = da[...]
        examples[pl.ds(at(3, rows // 2), rows // 2), :] = db[...]

    @pl.when(step == 0)
    def _():
        total[...] = jnp.zeros_like(total)

    @pl.when(step < half)
    def _():
        fill(mine, next_y, next_z, diag_a, diag_b)

    @pl.when(step >= half)
    def _():
        fill(*other)

    which = jnp.where(step < half, core, 1 - core)
    inner = jnp.where(step < half, step, step - half)
    row_start = (chip * 2 + which) * (half * depth) + inner * depth
    wide = 512
    held = examples[...]

    def chunk(index, carry):
        lane = lax.broadcasted_iota(jnp.int32, (1, wide), 1)
        cols = lane + (lane >> 8) * (2048 - 256) + (index * (wide // 256) * 2048 + slice_id * 256)
        table = signs(words, row_start, depth, cols)
        at = pl.ds(pl.multiple_of(index * wide, wide), wide)
        total[:, at] += jnp.dot(held, table, preferred_element_type=F32)
        return carry

    lax.fori_loop(0, total.shape[1] // wide, chunk, 0, unroll=2)

    @pl.when(step == 2 * half - 1)
    def _():
        for block in range(8):
            out[block] = total[:, block * 256 : (block + 1) * 256] * SCALE


def project(words, own, other, depth=512):
    rows, params = own[0].shape
    half = params // depth

    def spec(array, second):
        if second:
            return pl.BlockSpec((array.shape[0], depth), lambda k: (0, jnp.maximum(k - half, 0)))
        return pl.BlockSpec((array.shape[0], depth), lambda k: (0, jnp.minimum(k, half - 1)))

    return pl.pallas_call(
        project_kernel,
        out_shape=jax.ShapeDtypeStruct((8, 4 * rows, 256), F32),
        grid=(2 * half,),
        in_specs=[pl.BlockSpec(memory_space=pltpu.SMEM)]
        + [spec(a, False) for a in own]
        + [spec(a, True) for a in other],
        out_specs=pl.BlockSpec((8, 4 * rows, 256), lambda k: (0, 0, 0)),
        scratch_shapes=[pltpu.VMEM((4 * rows, depth), BF16), pltpu.VMEM((4 * rows, 2048), F32)],
        compiler_params=pltpu.CompilerParams(vmem_limit_bytes=24 << 20),
        cost_estimate=pl.CostEstimate(flops=2 * 256 * 8192 * 2048, bytes_accessed=5 << 20, transcendentals=0),
    )(words, *own, *other)


def sum_kernel(parts, out):
    total = parts[0]
    for index in range(1, parts.shape[0]):
        total += parts[index]
    out[...] = total.astype(out.dtype)


def sum_parts(parts):
    return pl.pallas_call(
        sum_kernel,
        out_shape=jax.ShapeDtypeStruct(parts.shape[1:], BF16),
        compiler_params=pltpu.CompilerParams(vmem_limit_bytes=16 << 20),
    )(parts)


def condition_kernel(pieces, low, high, out):
    group = pl.program_id(0)
    total = None
    for yl in range(2):
        tile = (low, high)[yl]
        for zl in range(2):
            for core in range(2):
                start = (zl * 2 + core) * 256
                term = jnp.dot(
                    pieces[0, zl, yl, core], tile[start : start + 256, :], preferred_element_type=F32
                )
                total = term if total is None else total + term
    out[...] = total


def condition(pieces, low, high):
    rows = pieces.shape[4]
    return pl.pallas_call(
        condition_kernel,
        out_shape=jax.ShapeDtypeStruct((4 * rows, low.shape[1]), F32),
        grid=(4,),
        in_specs=[
            pl.BlockSpec((1,) + pieces.shape[1:], lambda g: (g, 0, 0, 0, 0, 0)),
            pl.BlockSpec(low.shape, lambda g: (0, 0)),
            pl.BlockSpec(high.shape, lambda g: (0, 0)),
        ],
        out_specs=pl.BlockSpec((rows, low.shape[1]), lambda g: (g, 0)),
        compiler_params=pltpu.CompilerParams(vmem_limit_bytes=24 << 20),
        cost_estimate=pl.CostEstimate(flops=2 * 512 * 2048 * 1024, bytes_accessed=7 << 20, transcendentals=0),
    )(pieces, low, high)


def pair_kernel(parts, features, out):
    total = parts[0]
    for index in range(1, parts.shape[0]):
        total += parts[index]
    rows = total.astype(BF16)
    for zh in range(4):
        pairs = None
        for zl in range(2):
            for core in range(2):
                start = (zl * 2 + core) * 256
                term = lax.dot_general(
                    rows[:, start : start + 256],
                    features[zh * 2 + zl, core],
                    (((1,), (1,)), ((), ())),
                    preferred_element_type=F32,
                )
                pairs = term if pairs is None else pairs + term
        for block in range(4):
            piece = pairs[:, block * 64 : (block + 1) * 64]
            out[zh * 4 + block, :, :64] = piece[:32]
            out[zh * 4 + block, :, 64:] = piece[32:]


def pair(parts, features):
    return pl.pallas_call(
        pair_kernel,
        out_shape=jax.ShapeDtypeStruct((16, 32, 128), F32),
        compiler_params=pltpu.CompilerParams(vmem_limit_bytes=24 << 20),
    )(parts, features)


def finish_kernel(parts, out):
    total = parts[0]
    for index in range(1, parts.shape[0]):
        total += parts[index]
    total = total * SCALE
    out[:32] = total[:, :64]
    out[32:] = total[:, 64:]


def finish(parts):
    return pl.pallas_call(
        finish_kernel,
        out_shape=jax.ShapeDtypeStruct((64, 64), F32),
    )(parts)


def swap(value, axis):
    return lax.ppermute(value, axis, [(0, 1), (1, 0)])


def per_device(gradients, inverse_gram, hash_words):
    core = lax.axis_index("c")
    half = gradients.shape[0] // 2
    next_y = swap(gradients, "yl")
    next_z = swap(gradients, "zl")
    own = [gradients, next_y, next_z, swap(next_y[:half], "zl"), swap(next_z[half:], "yl")]
    other = [swap(a, "c") for a in own]
    other_tile = swap(inverse_gram, "c")

    partial = project(hash_words, own, other)
    piece = sum_parts(lax.all_to_all(partial, CHIPS, 0, 0, tiled=True))

    by_core = jnp.transpose(piece.reshape(2, 2, 64, 256), (1, 0, 2, 3)).reshape(2, 128, 256)
    by_core = lax.all_to_all(by_core, "c", 0, 0, tiled=True)
    gathered = lax.all_gather(by_core, EX, axis=0).reshape(4, 2, 2, 2, 128, 256)

    route = []
    for z in range(8):
        for yl in range(2):
            for chip in range(8):
                for c in range(2):
                    route.append((((z * 2 + yl) * 8 + chip) * 2 + c, ((chip * 2 + yl) * 8 + z) * 2 + c))
    turned = lax.ppermute(piece, EX + PAR, route)
    features = lax.all_gather(turned, PAR, axis=0).reshape(8, 2, 256, 256)

    low = jnp.where(core == 0, inverse_gram, other_tile)
    high = jnp.where(core == 0, other_tile, inverse_gram)
    conditioned = condition(gathered, low, high)
    parts = lax.all_to_all(conditioned.reshape(8, 64, 1024), CHIPS, 0, 0, tiled=True)
    return finish(lax.all_to_all(pair(parts, features), EX, 0, 0, tiled=True))


def solution(mesh):
    fine = Mesh(mesh.devices.reshape(4, 2, 2, 2, 4, 2), EX + PAR)
    return jax.shard_map(
        per_device,
        mesh=fine,
        in_specs=(P(EX, PAR), P(PAR, EX), P()),
        out_specs=P(PAR, EX),
        check_vma=False,
    )
```

```python
import functools

import jax
import jax.numpy as jnp
from jax import lax
from jax.experimental import pallas as pl
from jax.experimental.pallas import tpu as pltpu
from jax.sharding import Mesh
from jax.sharding import PartitionSpec as P

FEATURES = 16384
SCALE = FEATURES ** (-0.5)
BF16 = jnp.bfloat16
F32 = jnp.float32

EX = ("zh", "zl", "yl")
CHIPS = ("yh", "x")
PAR = ("yh", "x", "c")


def shifted(values, amount):
    return lax.shift_right_logical(values, jnp.full(values.shape, amount, jnp.int32))


def signs(hash_words, row_start, rows, cols):
    m0 = hash_words[0] | 1
    row_ids = lax.broadcasted_iota(jnp.int32, (rows, cols.shape[1]), 0)
    mixed = row_ids * (FEATURES * m0) + (cols * m0 + (row_start * (FEATURES * m0) + hash_words[1]))
    mixed = mixed ^ shifted(mixed, 15)
    mixed = mixed * (hash_words[2] | 1)
    mixed = mixed ^ shifted(mixed, 13)
    mixed = mixed * (hash_words[3] | 1)
    return jnp.where(mixed < 0, BF16(-1), BF16(1))


def project_kernel(part, width, words, mine, next_y, next_z, diag_a, diag_b, *rest):
    other = rest[:5]
    out, examples, total = rest[5:]
    step = pl.program_id(0)
    half = pl.num_programs(0) // 2
    me = lax.axis_index("zl") * 2 + lax.axis_index("yl")
    core = lax.axis_index("c")
    chip = lax.axis_index("yh") * 4 + lax.axis_index("x")
    slice_id = lax.axis_index("yl") * 4 + lax.axis_index("zl") * 2 + core
    rows, depth = mine.shape

    def fill(own, y, z, da, db):
        def at(flip, offset=0):
            return pl.multiple_of((me ^ flip) * rows + offset, 32)

        examples[pl.ds(at(0), rows), :] = own[...]
        examples[pl.ds(at(1), rows), :] = y[...]
        examples[pl.ds(at(2), rows), :] = z[...]
        examples[pl.ds(at(3), rows // 2), :] = da[...]
        examples[pl.ds(at(3, rows // 2), rows // 2), :] = db[...]

    @pl.when(step == 0)
    def _():
        total[...] = jnp.zeros_like(total)

    @pl.when(step < half)
    def _():
        fill(mine, next_y, next_z, diag_a, diag_b)

    @pl.when(step >= half)
    def _():
        fill(*other)

    which = jnp.where(step < half, core, 1 - core)
    inner = jnp.where(step < half, step, step - half)
    row_start = (chip * 2 + which) * (half * depth) + inner * depth
    wide = 512
    held = examples[...]

    def chunk(index, carry):
        lane = lax.broadcasted_iota(jnp.int32, (1, wide), 1)
        group, within = lane // width, lane % width
        cols = (group + index * (wide // width)) * 2048 + within + (slice_id * 256 + part * width)
        table = signs(words, row_start, depth, cols)
        at = pl.ds(pl.multiple_of(index * wide, wide), wide)
        total[:, at] += jnp.dot(held, table, preferred_element_type=F32)
        return carry

    lax.fori_loop(0, total.shape[1] // wide, chunk, 0, unroll=2)

    @pl.when(step == 2 * half - 1)
    def _():
        for block in range(8):
            out[block] = total[:, block * width : (block + 1) * width] * SCALE


def project(part, width, words, own, other, depth=512):
    rows, params = own[0].shape
    half = params // depth

    def spec(array, second):
        if second:
            return pl.BlockSpec((array.shape[0], depth), lambda k: (0, jnp.maximum(k - half, 0)))
        return pl.BlockSpec((array.shape[0], depth), lambda k: (0, jnp.minimum(k, half - 1)))

    return pl.pallas_call(
        functools.partial(project_kernel, part, width),
        out_shape=jax.ShapeDtypeStruct((8, 4 * rows, width), F32),
        grid=(2 * half,),
        in_specs=[pl.BlockSpec(memory_space=pltpu.SMEM)]
        + [spec(a, False) for a in own]
        + [spec(a, True) for a in other],
        out_specs=pl.BlockSpec((8, 4 * rows, width), lambda k: (0, 0, 0)),
        scratch_shapes=[pltpu.VMEM((4 * rows, depth), BF16), pltpu.VMEM((4 * rows, 8 * width), F32)],
        compiler_params=pltpu.CompilerParams(vmem_limit_bytes=24 << 20),
        cost_estimate=pl.CostEstimate(flops=2 * 256 * 8192 * 8 * width, bytes_accessed=5 << 20, transcendentals=0),
    )(words, *own, *other)


def sum_kernel(*refs):
    parts, (whole, keep, send) = refs[:-3], refs[-3:]
    core = lax.axis_index("c")
    width = parts[0].shape[2]
    for run, part in enumerate(parts):
        at = slice(run * width, (run + 1) * width)
        total = part[0]
        for index in range(1, part.shape[0]):
            total += part[index]
        whole[:, at] = total.astype(BF16)
    for block in range(2):
        for target, which in ((keep, core), (send, 1 - core)):
            start = pl.multiple_of(block * 128 + which * 64, 64)
            target[block * 64 : (block + 1) * 64, :] = whole[pl.ds(start, 64), :]


def sum_parts(parts):
    rows = parts[0].shape[1]
    features = sum(p.shape[2] for p in parts)
    shapes = [(rows, features), (rows // 2, features), (rows // 2, features)]
    return pl.pallas_call(
        sum_kernel,
        out_shape=[jax.ShapeDtypeStruct(shape, BF16) for shape in shapes],
        compiler_params=pltpu.CompilerParams(vmem_limit_bytes=16 << 20),
    )(*parts)


def condition_kernel(pieces, mine, other, out):
    core = lax.axis_index("c")
    yl = lax.axis_index("yl")

    def run(near, far):
        total = None
        for zl in range(2):
            for flips in range(4):
                tile = (near, far)[flips // 2]
                start = pl.multiple_of((zl * 2 + (core ^ (flips % 2))) * 256, 256)
                term = jnp.dot(pieces[zl, flips], tile[pl.ds(start, 256), :], preferred_element_type=F32)
                total = term if total is None else total + term
        out[...] = total

    @pl.when(yl == core)
    def _():
        run(mine, other)

    @pl.when(yl != core)
    def _():
        run(other, mine)


def condition(pieces, mine, other):
    rows = pieces.shape[2]
    return pl.pallas_call(
        condition_kernel,
        out_shape=jax.ShapeDtypeStruct((4 * rows, mine.shape[1]), F32),
        grid=(4,),
        in_specs=[
            pl.BlockSpec((2,) + pieces.shape[1:], lambda g: (g, 0, 0, 0)),
            pl.BlockSpec(mine.shape, lambda g: (0, 0)),
            pl.BlockSpec(other.shape, lambda g: (0, 0)),
        ],
        out_specs=pl.BlockSpec((rows, mine.shape[1]), lambda g: (g, 0)),
        compiler_params=pltpu.CompilerParams(vmem_limit_bytes=24 << 20),
        cost_estimate=pl.CostEstimate(flops=2 * 512 * 2048 * 1024, bytes_accessed=7 << 20, transcendentals=0),
    )(pieces, mine, other)


def pair_kernel(parts, *refs):
    features, (out, rows, pairs) = refs[:8], refs[8:]
    yh, x, core = (lax.axis_index(name) for name in PAR)
    total = parts[0]
    for index in range(1, parts.shape[0]):
        total += parts[index]
    rows[...] = total.astype(BF16)
    pairs[...] = jnp.zeros_like(pairs)
    for shift in range(4):
        for flip_core in range(2):
            for flip_yh in range(2):
                z = (yh ^ flip_yh) * 4 + ((x + 4 - shift) & 3)
                start = pl.multiple_of(((z & 1) * 2 + (core ^ flip_core)) * 256, 256)
                at = pl.ds(pl.multiple_of((z >> 1) * 256, 256), 256)
                pairs[:, at] += lax.dot_general(
                    rows[:, pl.ds(start, 256)],
                    features[shift * 2 + flip_core][flip_yh],
                    (((1,), (1,)), ((), ())),
                    preferred_element_type=F32,
                )
    for block in range(16):
        piece = pairs[:, block * 64 : (block + 1) * 64]
        out[block, :, :64] = piece[:32]
        out[block, :, 64:] = piece[32:]


def pair(parts, features):
    return pl.pallas_call(
        pair_kernel,
        out_shape=jax.ShapeDtypeStruct((16, 32, 128), F32),
        scratch_shapes=[pltpu.VMEM((64, 1024), BF16), pltpu.VMEM((64, 1024), F32)],
        compiler_params=pltpu.CompilerParams(vmem_limit_bytes=24 << 20),
    )(parts, *features)


def finish_kernel(parts, out):
    total = parts[0]
    for index in range(1, parts.shape[0]):
        total += parts[index]
    total = total * SCALE
    out[:32] = total[:, :64]
    out[32:] = total[:, 64:]


def finish(parts):
    return pl.pallas_call(
        finish_kernel,
        out_shape=jax.ShapeDtypeStruct((64, 64), F32),
    )(parts)


def swap(value, axis):
    return lax.ppermute(value, axis, [(0, 1), (1, 0)])


def shift_x(value, by):
    return lax.ppermute(value, "x", [(i, (i + by) % 4) for i in range(4)])


def per_device(gradients, inverse_gram, hash_words):
    half = gradients.shape[0] // 2
    next_y = swap(gradients, "yl")
    next_z = swap(gradients, "zl")
    own = [gradients, next_y, next_z, swap(next_y[:half], "zl"), swap(next_z[half:], "yl")]
    other = [swap(a, "c") for a in own]
    other_tile = swap(inverse_gram, "c")

    runs = []
    for part in range(2):
        partial = project(part, 128, hash_words, own, other)
        runs.append(lax.all_to_all(partial, CHIPS, 0, 0, tiled=True))
    whole, keep, send = sum_parts(runs)

    received = swap(send, "c")
    mine = jnp.stack([keep, received, swap(keep, "yl"), swap(received, "yl")])
    gathered = lax.all_gather(mine, ("zh", "zl"), axis=0)

    route = []
    for z in range(8):
        for yl in range(2):
            for chip in range(8):
                for c in range(2):
                    route.append((((z * 2 + yl) * 8 + chip) * 2 + c, ((chip * 2 + yl) * 8 + z) * 2 + c))
    turned = lax.ppermute(whole, EX + PAR, route)
    turned = jnp.stack([turned, swap(turned, "yh")])
    features = []
    for by in range(4):
        shifted_x = shift_x(turned, by) if by else turned
        features += [shifted_x, swap(shifted_x, "c")]

    gathered, features = lax.optimization_barrier((gathered, features))
    conditioned = condition(gathered, inverse_gram, other_tile)
    parts = lax.all_to_all(conditioned.reshape(8, 64, 1024), CHIPS, 0, 0, tiled=True)
    return finish(lax.all_to_all(pair(parts, features), EX, 0, 0, tiled=True))


def solution(mesh):
    fine = Mesh(mesh.devices.reshape(4, 2, 2, 2, 4, 2), EX + PAR)
    return jax.shard_map(
        per_device,
        mesh=fine,
        in_specs=(P(EX, PAR), P(PAR, EX), P()),
        out_specs=P(PAR, EX),
        check_vma=False,
    )
```

```python
import functools

import jax
import jax.numpy as jnp
from jax import lax
from jax.experimental import pallas as pl
from jax.experimental.pallas import tpu as pltpu
from jax.sharding import Mesh
from jax.sharding import PartitionSpec as P

FEATURES = 16384
SCALE = FEATURES ** (-0.5)
BF16 = jnp.bfloat16
F32 = jnp.float32

EX = ("zh", "zl", "yl")
CHIPS = ("yh", "x")
PAR = ("yh", "x", "c")
FEATURES_PER_CHIP = FEATURES // 8


def shifted(values, amount):
    return lax.shift_right_logical(values, jnp.full(values.shape, amount, jnp.int32))


def signs(hash_words, row_start, rows, cols):
    m0 = hash_words[0] | 1
    row_ids = lax.broadcasted_iota(jnp.int32, (rows, cols.shape[1]), 0)
    mixed = row_ids * (FEATURES * m0) + (cols * m0 + (row_start * (FEATURES * m0) + hash_words[1]))
    mixed = mixed ^ shifted(mixed, 15)
    mixed = mixed * (hash_words[2] | 1)
    mixed = mixed ^ shifted(mixed, 13)
    mixed = mixed * (hash_words[3] | 1)
    return jnp.where(mixed < 0, BF16(-1), BF16(1))


def columns(first, count, part, width):
    slice_id = lax.axis_index("yl") * 4 + lax.axis_index("zl") * 2 + lax.axis_index("c")
    column = lax.broadcasted_iota(jnp.int32, (1, count), 1)
    group, within = column // width, column % width
    return (group + first // width) * FEATURES_PER_CHIP + within + (slice_id * 256 + part * width)


def first_parameter(block, depth, params):
    per_core = params // 2 // depth
    core = lax.axis_index("c")
    chip = lax.axis_index("yh") * 4 + lax.axis_index("x")
    which = jnp.where(block < per_core, core, 1 - core)
    inner = jnp.where(block < per_core, block, block - per_core)
    return (chip * 2 + which) * (params // 2) + inner * depth


def table_kernel(part, width, first, params, words, out):
    depth, wide = out.shape
    row_start = first_parameter(pl.program_id(0) + first, depth, params)
    rows = 32

    def chunk(index, carry):
        start = pl.multiple_of(index * rows, rows)
        cols = columns(0, wide, part, width)
        out[pl.ds(start, rows), :] = signs(words, row_start + start, rows, cols)
        return carry

    lax.fori_loop(0, depth // rows, chunk, 0)


def table(part, width, first, count, depth, params, words):
    return pl.pallas_call(
        functools.partial(table_kernel, part, width, first, params),
        out_shape=jax.ShapeDtypeStruct((count * depth, 8 * width), BF16),
        grid=(count,),
        in_specs=[pl.BlockSpec(memory_space=pltpu.SMEM)],
        out_specs=pl.BlockSpec((depth, 8 * width), lambda k: (k, 0)),
        compiler_params=pltpu.CompilerParams(vmem_limit_bytes=60 << 20),
        cost_estimate=pl.CostEstimate(
            flops=1200 * count * depth * 8 * width,
            bytes_accessed=2 * count * depth * 8 * width,
            transcendentals=0,
        ),
    )(words)


def load_examples(blocks, examples, arrived):
    me = lax.axis_index("zl") * 2 + lax.axis_index("yl")
    half = len(blocks) // 2
    params = blocks[0].shape[1]
    rows = blocks[0].shape[0]
    copies = []
    for index, block in enumerate(blocks):
        kind = index % half
        start = (me ^ min(kind, 3)) * rows + (rows // 2 if kind == 4 else 0)
        target = examples.at[
            pl.ds(pl.multiple_of(start, 32), block.shape[0]),
            (index // half) * params : (index // half + 1) * params,
        ]
        copies.append(pltpu.make_async_copy(block, target, arrived.at[index]))
    for copy in copies:
        copy.start()
    for copy in copies:
        copy.wait()


def write_run(out, total, width):
    for block in range(8):
        out[block] = total[:, block * width : (block + 1) * width] * SCALE


def ready_kernel(split, width, first, second, *refs):
    blocks, (out, examples, total, arrived) = refs[:-4], refs[-4:]
    step = pl.program_id(0)
    depth = first.shape[0]

    @pl.when(step == 0)
    def _():
        load_examples(blocks, examples, arrived)
        total[...] = jnp.zeros_like(total)

    held = examples[:, pl.ds(pl.multiple_of(step * depth, depth), depth)]

    @pl.when(step < split)
    def _():
        total[...] += jnp.dot(held, first[...], preferred_element_type=F32)

    @pl.when(step >= split)
    def _():
        total[...] += jnp.dot(held, second[...], preferred_element_type=F32)

    @pl.when(step == pl.num_programs(0) - 1)
    def _():
        write_run(out, total, width)


def hash_kernel(part, width, words, *refs):
    blocks, (out, examples, total, arrived) = refs[:-4], refs[-4:]
    step = pl.program_id(0)
    params = examples.shape[1]
    depth = params // pl.num_programs(0)
    wide = 512

    @pl.when(step == 0)
    def _():
        load_examples(blocks, examples, arrived)
        total[...] = jnp.zeros_like(total)

    held = examples[:, pl.ds(pl.multiple_of(step * depth, depth), depth)]
    row_start = first_parameter(step, depth, params)
    for first in range(0, 8 * width, wide):
        made = signs(words, row_start, depth, columns(first, wide, part, width))
        total[:, first : first + wide] += jnp.dot(held, made, preferred_element_type=F32)

    @pl.when(step == pl.num_programs(0) - 1)
    def _():
        write_run(out, total, width)


def project(kernel, leading, specs, steps, width, blocks):
    rows, params = 4 * blocks[0].shape[0], 2 * blocks[0].shape[1]
    return pl.pallas_call(
        kernel,
        out_shape=jax.ShapeDtypeStruct((8, rows, width), F32),
        grid=(steps,),
        in_specs=specs + [pl.BlockSpec(memory_space=pltpu.HBM)] * len(blocks),
        out_specs=pl.BlockSpec((8, rows, width), lambda k: (0, 0, 0)),
        scratch_shapes=[
            pltpu.VMEM((rows, params), BF16),
            pltpu.VMEM((rows, 8 * width), F32),
            pltpu.SemaphoreType.DMA((len(blocks),)),
        ],
        compiler_params=pltpu.CompilerParams(vmem_limit_bytes=60 << 20),
        cost_estimate=pl.CostEstimate(
            flops=2 * rows * params * 8 * width, bytes_accessed=16 << 20, transcendentals=0
        ),
    )(*leading, *blocks)


def sum_kernel(part, *earlier_and_outs):
    earlier, (whole, keep, send) = earlier_and_outs[:-3], earlier_and_outs[-3:]
    core = lax.axis_index("c")
    width = part.shape[2]
    total = part[0]
    for index in range(1, part.shape[0]):
        total += part[index]
    total = total.astype(BF16)
    for index, value in enumerate(earlier):
        whole[:, index * width : (index + 1) * width] = value[...]
    whole[:, len(earlier) * width :] = total
    mine = slice(len(earlier) * width, (len(earlier) + 1) * width)
    for block in range(2):
        for target, which in ((keep, core), (send, 1 - core)):
            start = pl.multiple_of(block * 128 + which * 64, 64)
            target[block * 64 : (block + 1) * 64, :] = whole[pl.ds(start, 64), mine]


def sum_parts(part, *earlier):
    _, rows, width = part.shape
    shapes = [(rows, width * (1 + len(earlier))), (rows // 2, width), (rows // 2, width)]
    return pl.pallas_call(
        sum_kernel,
        out_shape=[jax.ShapeDtypeStruct(shape, BF16) for shape in shapes],
        compiler_params=pltpu.CompilerParams(vmem_limit_bytes=8 << 20),
    )(part, *earlier)


def condition_kernel(low, high, mine, other, out):
    core = lax.axis_index("c")
    yl = lax.axis_index("yl")

    def run(near, far):
        total = None
        for zl in range(2):
            for flips in range(4):
                tile = (near, far)[flips // 2]
                start = pl.multiple_of((zl * 2 + (core ^ (flips % 2))) * 256, 256)
                piece = jnp.concatenate([low[zl, flips], high[zl, flips]], axis=1)
                term = jnp.dot(piece, tile[pl.ds(start, 256), :], preferred_element_type=F32)
                total = term if total is None else total + term
        out[...] = total

    @pl.when(yl == core)
    def _():
        run(mine, other)

    @pl.when(yl != core)
    def _():
        run(other, mine)


def condition(low, high, mine, other):
    rows = low.shape[2]
    return pl.pallas_call(
        condition_kernel,
        out_shape=jax.ShapeDtypeStruct((4 * rows, mine.shape[1]), F32),
        grid=(4,),
        in_specs=[
            pl.BlockSpec((2,) + low.shape[1:], lambda g: (g, 0, 0, 0)),
            pl.BlockSpec((2,) + high.shape[1:], lambda g: (g, 0, 0, 0)),
            pl.BlockSpec(mine.shape, lambda g: (0, 0)),
            pl.BlockSpec(other.shape, lambda g: (0, 0)),
        ],
        out_specs=pl.BlockSpec((rows, mine.shape[1]), lambda g: (g, 0)),
        compiler_params=pltpu.CompilerParams(vmem_limit_bytes=24 << 20),
        cost_estimate=pl.CostEstimate(flops=2 * 512 * 2048 * 1024, bytes_accessed=7 << 20, transcendentals=0),
    )(low, high, mine, other)


def pair_kernel(parts, *refs):
    away, (out, rows, pairs, features, arrived) = refs[:8], refs[8:]
    copies = [pltpu.make_async_copy(a, features.at[i], arrived.at[i]) for i, a in enumerate(away)]
    for copy in copies:
        copy.start()
    yh, x, core = (lax.axis_index(name) for name in PAR)
    total = parts[0]
    for index in range(1, parts.shape[0]):
        total += parts[index]
    rows[...] = total.astype(BF16)
    pairs[...] = jnp.zeros_like(pairs)
    for copy in copies:
        copy.wait()
    for shift in range(4):
        for flip_core in range(2):
            for flip_yh in range(2):
                z = (yh ^ flip_yh) * 4 + ((x + 4 - shift) & 3)
                start = pl.multiple_of(((z & 1) * 2 + (core ^ flip_core)) * 256, 256)
                at = pl.ds(pl.multiple_of((z >> 1) * 256, 256), 256)
                pairs[:, at] += lax.dot_general(
                    rows[:, pl.ds(start, 256)],
                    features[shift * 2 + flip_core, flip_yh],
                    (((1,), (1,)), ((), ())),
                    preferred_element_type=F32,
                )
    for block in range(16):
        piece = pairs[:, block * 64 : (block + 1) * 64]
        out[block, :, :64] = piece[:32]
        out[block, :, 64:] = piece[32:]


def pair(parts, features):
    return pl.pallas_call(
        pair_kernel,
        out_shape=jax.ShapeDtypeStruct((16, 32, 128), F32),
        in_specs=[pl.BlockSpec(memory_space=pltpu.VMEM)] + [pl.BlockSpec(memory_space=pltpu.HBM)] * 8,
        scratch_shapes=[
            pltpu.VMEM((64, 1024), BF16),
            pltpu.VMEM((64, 1024), F32),
            pltpu.VMEM((8, 2, 256, 256), BF16),
            pltpu.SemaphoreType.DMA((8,)),
        ],
        compiler_params=pltpu.CompilerParams(vmem_limit_bytes=60 << 20),
    )(parts, *features)


def finish_kernel(parts, out):
    total = parts[0]
    for index in range(1, parts.shape[0]):
        total += parts[index]
    total = total * SCALE
    out[:32] = total[:, :64]
    out[32:] = total[:, 64:]


def finish(parts):
    return pl.pallas_call(
        finish_kernel,
        out_shape=jax.ShapeDtypeStruct((64, 64), F32),
    )(parts)


def swap(value, axis):
    return lax.ppermute(value, axis, [(0, 1), (1, 0)])


def shift_x(value, by):
    return lax.ppermute(value, "x", [(i, (i + by) % 4) for i in range(4)])


def per_device(gradients, inverse_gram, hash_words):
    half = gradients.shape[0] // 2
    next_y = swap(gradients, "yl")
    next_z = swap(gradients, "zl")
    own = [gradients, next_y, next_z, swap(next_y[:half], "zl"), swap(next_z[half:], "yl")]
    other = [swap(a, "c") for a in own]
    other_tile = swap(inverse_gram, "c")

    blocks = own + other
    width, depth, params = 128, 1024, 2 * gradients.shape[1]
    split = 5
    words_spec = pl.BlockSpec(memory_space=pltpu.SMEM)

    first = table(0, width, 0, split, depth, params, hash_words)
    second = table(0, width, split, params // depth - split, depth, params, hash_words)
    table_specs = [
        pl.BlockSpec((depth, 8 * width), lambda k: (jnp.minimum(k, split - 1), 0)),
        pl.BlockSpec((depth, 8 * width), lambda k: (jnp.maximum(k - split, 0), 0)),
    ]
    partial = project(
        functools.partial(ready_kernel, split, width), [first, second], table_specs, params // depth, width, blocks
    )
    part = lax.all_to_all(partial, CHIPS, 0, 0, tiled=True)
    partial = project(functools.partial(hash_kernel, 1, width), [hash_words], [words_spec], 16, width, blocks)
    partial, part = lax.optimization_barrier((partial, part))
    next_part = lax.all_to_all(partial, CHIPS, 0, 0, tiled=True)

    def flips(keep, send):
        received = swap(send, "c")
        return jnp.stack([keep, received, swap(keep, "yl"), swap(received, "yl")])

    whole, keep, send = sum_parts(part)
    mine = flips(keep, send)
    low = lax.all_gather(mine, ("zh", "zl"), axis=0)
    next_part, mine = lax.optimization_barrier((next_part, mine))
    whole, keep, send = sum_parts(next_part, whole)
    mine, low = lax.optimization_barrier((flips(keep, send), low))
    high = lax.all_gather(mine, ("zh", "zl"), axis=0)

    route = []
    for z in range(8):
        for yl in range(2):
            for chip in range(8):
                for c in range(2):
                    route.append((((z * 2 + yl) * 8 + chip) * 2 + c, ((chip * 2 + yl) * 8 + z) * 2 + c))
    turned = lax.ppermute(whole, EX + PAR, route)
    turned = jnp.stack([turned, swap(turned, "yh")])
    features = []
    for by in range(4):
        shifted_x = shift_x(turned, by) if by else turned
        features += [shifted_x, swap(shifted_x, "c")]

    high, features = lax.optimization_barrier((high, features))
    conditioned = condition(low, high, inverse_gram, other_tile)
    parts = lax.all_to_all(conditioned.reshape(8, 64, 1024), CHIPS, 0, 0, tiled=True)
    return finish(lax.all_to_all(pair(parts, features), EX, 0, 0, tiled=True))


def solution(mesh):
    fine = Mesh(mesh.devices.reshape(4, 2, 2, 2, 4, 2), EX + PAR)
    return jax.shard_map(
        per_device,
        mesh=fine,
        in_specs=(P(EX, PAR), P(PAR, EX), P()),
        out_specs=P(PAR, EX),
        check_vma=False,
    )
```

```python
import functools

import jax
import jax.numpy as jnp
from jax import lax
from jax.experimental import pallas as pl
from jax.experimental.pallas import tpu as pltpu
from jax.sharding import Mesh
from jax.sharding import PartitionSpec as P

FEATURES = 16384
SCALE = FEATURES ** (-0.5)
BF16 = jnp.bfloat16
F32 = jnp.float32

EX = ("zh", "zl", "yl")
CHIPS = ("yh", "x")
PAR = ("yh", "x", "c")
FEATURES_PER_CHIP = FEATURES // 8


def shifted(values, amount):
    return lax.shift_right_logical(values, jnp.full(values.shape, amount, jnp.int32))


def signs(hash_words, row_start, rows, cols):
    m0 = hash_words[0] | 1
    row_ids = lax.broadcasted_iota(jnp.int32, (rows, cols.shape[1]), 0)
    mixed = row_ids * (FEATURES * m0) + (cols * m0 + (row_start * (FEATURES * m0) + hash_words[1]))
    mixed = mixed ^ shifted(mixed, 15)
    mixed = mixed * (hash_words[2] | 1)
    mixed = mixed ^ shifted(mixed, 13)
    mixed = mixed * (hash_words[3] | 1)
    return jnp.where(mixed < 0, BF16(-1), BF16(1))


def columns(first, count, part, width):
    slice_id = lax.axis_index("yl") * 4 + lax.axis_index("zl") * 2 + lax.axis_index("c")
    column = lax.broadcasted_iota(jnp.int32, (1, count), 1)
    group, within = column // width, column % width
    return (group + first // width) * FEATURES_PER_CHIP + within + (slice_id * 256 + part * width)


def first_parameter(block, depth, params):
    per_core = params // 2 // depth
    core = lax.axis_index("c")
    chip = lax.axis_index("yh") * 4 + lax.axis_index("x")
    which = jnp.where(block < per_core, core, 1 - core)
    inner = jnp.where(block < per_core, block, block - per_core)
    return (chip * 2 + which) * (params // 2) + inner * depth


def table_kernel(part, width, first, params, words, out):
    depth, wide = out.shape
    row_start = first_parameter(pl.program_id(0) + first, depth, params)
    rows = 32

    def chunk(index, carry):
        start = pl.multiple_of(index * rows, rows)
        cols = columns(0, wide, part, width)
        out[pl.ds(start, rows), :] = signs(words, row_start + start, rows, cols)
        return carry

    lax.fori_loop(0, depth // rows, chunk, 0)


def table(part, width, first, count, depth, params, words):
    return pl.pallas_call(
        functools.partial(table_kernel, part, width, first, params),
        out_shape=jax.ShapeDtypeStruct((count * depth, 8 * width), BF16),
        grid=(count,),
        in_specs=[pl.BlockSpec(memory_space=pltpu.SMEM)],
        out_specs=pl.BlockSpec((depth, 8 * width), lambda k: (k, 0)),
        compiler_params=pltpu.CompilerParams(vmem_limit_bytes=12 << 20),
        cost_estimate=pl.CostEstimate(
            flops=1200 * count * depth * 8 * width,
            bytes_accessed=2 * count * depth * 8 * width,
            transcendentals=0,
        ),
    )(words)


def load_examples(blocks, examples, arrived):
    me = lax.axis_index("zl") * 2 + lax.axis_index("yl")
    half = len(blocks) // 2
    params = blocks[0].shape[1]
    rows = blocks[0].shape[0]
    copies = []
    for index, block in enumerate(blocks):
        kind = index % half
        start = (me ^ min(kind, 3)) * rows + (rows // 2 if kind == 4 else 0)
        target = examples.at[
            pl.ds(pl.multiple_of(start, 32), block.shape[0]),
            (index // half) * params : (index // half + 1) * params,
        ]
        copies.append(pltpu.make_async_copy(block, target, arrived.at[index]))
    for copy in copies:
        copy.start()
    for copy in copies:
        copy.wait()


def write_run(out, total, width):
    for block in range(8):
        out[block] = total[:, block * width : (block + 1) * width] * SCALE


def ready_kernel(split, width, first, second, *refs):
    blocks, (out, examples, total, arrived) = refs[:-4], refs[-4:]
    step = pl.program_id(0)
    depth = first.shape[0]

    @pl.when(step == 0)
    def _():
        load_examples(blocks, examples, arrived)
        total[...] = jnp.zeros_like(total)

    held = examples[:, pl.ds(pl.multiple_of(step * depth, depth), depth)]

    @pl.when(step < split)
    def _():
        total[...] += jnp.dot(held, first[...], preferred_element_type=F32)

    @pl.when(step >= split)
    def _():
        total[...] += jnp.dot(held, second[...], preferred_element_type=F32)

    @pl.when(step == pl.num_programs(0) - 1)
    def _():
        write_run(out, total, width)


def hash_kernel(part, width, words, *refs):
    blocks, (out, examples, total, arrived) = refs[:-4], refs[-4:]
    step = pl.program_id(0)
    params = examples.shape[1]
    depth = params // pl.num_programs(0)
    wide = 512

    @pl.when(step == 0)
    def _():
        load_examples(blocks, examples, arrived)
        total[...] = jnp.zeros_like(total)

    held = examples[:, pl.ds(pl.multiple_of(step * depth, depth), depth)]
    row_start = first_parameter(step, depth, params)
    for first in range(0, 8 * width, wide):
        made = signs(words, row_start, depth, columns(first, wide, part, width))
        total[:, first : first + wide] += jnp.dot(held, made, preferred_element_type=F32)

    @pl.when(step == pl.num_programs(0) - 1)
    def _():
        write_run(out, total, width)


def project(kernel, leading, specs, steps, width, blocks, vmem):
    rows, params = 4 * blocks[0].shape[0], 2 * blocks[0].shape[1]
    return pl.pallas_call(
        kernel,
        out_shape=jax.ShapeDtypeStruct((8, rows, width), F32),
        grid=(steps,),
        in_specs=specs + [pl.BlockSpec(memory_space=pltpu.HBM)] * len(blocks),
        out_specs=pl.BlockSpec((8, rows, width), lambda k: (0, 0, 0)),
        scratch_shapes=[
            pltpu.VMEM((rows, params), BF16),
            pltpu.VMEM((rows, 8 * width), F32),
            pltpu.SemaphoreType.DMA((len(blocks),)),
        ],
        compiler_params=pltpu.CompilerParams(vmem_limit_bytes=vmem << 20),
        cost_estimate=pl.CostEstimate(
            flops=2 * rows * params * 8 * width, bytes_accessed=16 << 20, transcendentals=0
        ),
    )(*leading, *blocks)


def sum_kernel(part, *earlier_and_outs):
    earlier, (whole, keep, send) = earlier_and_outs[:-3], earlier_and_outs[-3:]
    core = lax.axis_index("c")
    width = part.shape[2]
    total = part[0]
    for index in range(1, part.shape[0]):
        total += part[index]
    total = total.astype(BF16)
    for index, value in enumerate(earlier):
        whole[:, index * width : (index + 1) * width] = value[...]
    whole[:, len(earlier) * width :] = total
    mine = slice(len(earlier) * width, (len(earlier) + 1) * width)
    for block in range(2):
        for target, which in ((keep, core), (send, 1 - core)):
            start = pl.multiple_of(block * 128 + which * 64, 64)
            target[block * 64 : (block + 1) * 64, :] = whole[pl.ds(start, 64), mine]


def sum_parts(part, *earlier):
    _, rows, width = part.shape
    shapes = [(rows, width * (1 + len(earlier))), (rows // 2, width), (rows // 2, width)]
    return pl.pallas_call(
        sum_kernel,
        out_shape=[jax.ShapeDtypeStruct(shape, BF16) for shape in shapes],
        compiler_params=pltpu.CompilerParams(vmem_limit_bytes=8 << 20),
    )(part, *earlier)


RING = (0, -1, -2, -3, -4, 1, 2, 3)


def condition_kernel(*refs):
    runs, (mine, other), (out, pieces, tiles, arrived) = (refs[:8], refs[8:16]), refs[16:18], refs[18:]
    core = lax.axis_index("c")
    yl = lax.axis_index("yl")
    z = lax.axis_index("zh") * 2 + lax.axis_index("zl")
    first = [
        pltpu.make_async_copy(mine, tiles.at[core], arrived.at[16]),
        pltpu.make_async_copy(other, tiles.at[1 - core], arrived.at[17]),
    ]
    copies = []
    for index in range(8):
        for run in range(2):
            target = pieces.at[index, :, :, run * 128 : (run + 1) * 128]
            copies.append(pltpu.make_async_copy(runs[run][index], target, arrived.at[index * 2 + run]))
    for copy in first + copies:
        copy.start()
    out[...] = jnp.zeros_like(out)
    for copy in first:
        copy.wait()
    for index, away in enumerate(RING):
        copies[index * 2].wait()
        copies[index * 2 + 1].wait()
        source = (z + (away + 8)) & 7
        total = None
        for flip in range(4):
            start = pl.multiple_of(((source & 1) * 2 + (core ^ (flip % 2))) * 256, 256)
            tile = tiles[yl ^ (flip // 2), pl.ds(start, 256), :]
            term = jnp.dot(pieces[index, flip], tile, preferred_element_type=F32)
            total = term if total is None else total + term
        out[pl.ds(pl.multiple_of((source >> 1) * 128, 128), 128), :] += total


def condition(low, high, mine, other):
    flips, rows, width = low[0].shape
    return pl.pallas_call(
        condition_kernel,
        out_shape=jax.ShapeDtypeStruct((4 * rows, mine.shape[1]), F32),
        in_specs=[pl.BlockSpec(memory_space=pltpu.HBM)] * 18,
        out_specs=pl.BlockSpec(memory_space=pltpu.VMEM),
        scratch_shapes=[
            pltpu.VMEM((8, flips, rows, 2 * width), BF16),
            pltpu.VMEM((2,) + mine.shape, BF16),
            pltpu.SemaphoreType.DMA((18,)),
        ],
        compiler_params=pltpu.CompilerParams(vmem_limit_bytes=24 << 20),
        cost_estimate=pl.CostEstimate(flops=2 * 512 * 2048 * 1024, bytes_accessed=7 << 20, transcendentals=0),
    )(*low, *high, mine, other)


def pair_kernel(parts, near, far, out, rows, pairs):
    core = lax.axis_index("c")
    total = parts[0]
    for index in range(1, parts.shape[0]):
        total += parts[index]
    rows[...] = total.astype(BF16)
    for zh in range(4):
        value = None
        for zl in range(2):
            for flip in range(2):
                start = pl.multiple_of((zl * 2 + (core ^ flip)) * 256, 256)
                term = lax.dot_general(
                    rows[:, pl.ds(start, 256)],
                    (near, far)[flip][zh * 2 + zl],
                    (((1,), (1,)), ((), ())),
                    preferred_element_type=F32,
                )
                value = term if value is None else value + term
        pairs[:, zh * 256 : (zh + 1) * 256] = value
    for block in range(16):
        piece = pairs[:, block * 64 : (block + 1) * 64]
        out[block, :, :64] = piece[:32]
        out[block, :, 64:] = piece[32:]


def pair(parts, near, far):
    return pl.pallas_call(
        pair_kernel,
        out_shape=jax.ShapeDtypeStruct((16, 32, 128), F32),
        scratch_shapes=[pltpu.VMEM((64, 1024), BF16), pltpu.VMEM((64, 1024), F32)],
        compiler_params=pltpu.CompilerParams(vmem_limit_bytes=12 << 20),
    )(parts, near, far)


def finish_kernel(parts, out):
    total = parts[0]
    for index in range(1, parts.shape[0]):
        total += parts[index]
    total = total * SCALE
    out[:32] = total[:, :64]
    out[32:] = total[:, 64:]


def finish(parts):
    return pl.pallas_call(
        finish_kernel,
        out_shape=jax.ShapeDtypeStruct((64, 64), F32),
    )(parts)


def swap(value, axis):
    return lax.ppermute(value, axis, [(0, 1), (1, 0)])


def ring(value):
    up, down = [], []
    ahead = behind = value
    for step in range(4):
        ahead = lax.ppermute(ahead, ("zh", "zl"), [(i, (i + 1) % 8) for i in range(8)])
        up.append(ahead)
        if step < 3:
            behind = lax.ppermute(behind, ("zh", "zl"), [(i, (i + 7) % 8) for i in range(8)])
            down.append(behind)
    return [value] + up + down


def flips(keep, send):
    received = swap(send, "c")
    return jnp.stack([keep, received, swap(keep, "yl"), swap(received, "yl")])


def per_device(gradients, inverse_gram, hash_words):
    half = gradients.shape[0] // 2
    width, depth, params = 128, 1024, 2 * gradients.shape[1]
    split = 5
    words_spec = pl.BlockSpec(memory_space=pltpu.SMEM)
    first = table(0, width, 0, split, depth, params, hash_words)
    second = table(0, width, split, params // depth - split, depth, params, hash_words)

    next_y = swap(gradients, "yl")
    next_z = swap(gradients, "zl")
    first, next_y, next_z = lax.optimization_barrier((first, next_y, next_z))
    own = [gradients, next_y, next_z, swap(next_y[:half], "zl"), swap(next_z[half:], "yl")]
    blocks = own + [swap(a, "c") for a in own]
    other_tile = swap(inverse_gram, "c")

    table_specs = [
        pl.BlockSpec((depth, 8 * width), lambda k: (jnp.minimum(k, split - 1), 0)),
        pl.BlockSpec((depth, 8 * width), lambda k: (jnp.maximum(k - split, 0), 0)),
    ]
    partial = project(
        functools.partial(ready_kernel, split, width), [first, second], table_specs, params // depth, width, blocks, 24
    )
    part = lax.all_to_all(partial, CHIPS, 0, 0, tiled=True)
    partial = project(functools.partial(hash_kernel, 1, width), [hash_words], [words_spec], 16, width, blocks, 60)
    partial, part = lax.optimization_barrier((partial, part))
    next_part = lax.all_to_all(partial, CHIPS, 0, 0, tiled=True)

    whole, keep, send = sum_parts(part)
    low = ring(flips(keep, send))
    next_part, low = lax.optimization_barrier((next_part, low))
    whole, keep, send = sum_parts(next_part, whole)
    whole, mine = lax.optimization_barrier((whole, flips(keep, send)))
    high = ring(mine)

    route = []
    for z in range(8):
        for yl in range(2):
            for chip in range(8):
                for c in range(2):
                    route.append((((z * 2 + yl) * 8 + chip) * 2 + c, ((chip * 2 + yl) * 8 + z) * 2 + c))
    turned = lax.ppermute(whole, EX + PAR, route)
    near = lax.all_gather(turned, CHIPS, axis=0)
    far = swap(near, "c")

    conditioned = condition(low, high, inverse_gram, other_tile)
    parts = lax.all_to_all(conditioned.reshape(8, 64, 1024), CHIPS, 0, 0, tiled=True)
    return finish(lax.all_to_all(pair(parts, near, far), EX, 0, 0, tiled=True))


def solution(mesh):
    fine = Mesh(mesh.devices.reshape(4, 2, 2, 2, 4, 2), EX + PAR)
    return jax.shard_map(
        per_device,
        mesh=fine,
        in_specs=(P(EX, PAR), P(PAR, EX), P()),
        out_specs=P(PAR, EX),
        check_vma=False,
    )
```

```python
import functools

import jax
import jax.numpy as jnp
from jax import lax
from jax.experimental import pallas as pl
from jax.experimental.pallas import tpu as pltpu
from jax.sharding import Mesh
from jax.sharding import PartitionSpec as P

FEATURES = 16384
SCALE = FEATURES ** (-0.5)
BF16 = jnp.bfloat16
F32 = jnp.float32

EX = ("zh", "zl", "yl")
CHIPS = ("yh", "x")
PAR = ("yh", "x", "c")
FEATURES_PER_CHIP = FEATURES // 8


def shifted(values, amount):
    return lax.shift_right_logical(values, jnp.full(values.shape, amount, jnp.int32))


def signs(hash_words, row_start, rows, cols):
    m0 = hash_words[0] | 1
    row_ids = lax.broadcasted_iota(jnp.int32, (rows, cols.shape[1]), 0)
    mixed = row_ids * (FEATURES * m0) + (cols * m0 + (row_start * (FEATURES * m0) + hash_words[1]))
    mixed = mixed ^ shifted(mixed, 15)
    mixed = mixed * (hash_words[2] | 1)
    mixed = mixed ^ shifted(mixed, 13)
    mixed = mixed * (hash_words[3] | 1)
    return jnp.where(mixed < 0, BF16(-1), BF16(1))


def columns(first, count, part, width):
    slice_id = lax.axis_index("yl") * 4 + lax.axis_index("zl") * 2 + lax.axis_index("c")
    column = lax.broadcasted_iota(jnp.int32, (1, count), 1)
    group, within = column // width, column % width
    return (group + first // width) * FEATURES_PER_CHIP + within + (slice_id * 256 + part * width)


def first_parameter(block, depth, params):
    per_core = params // 2 // depth
    core = lax.axis_index("c")
    chip = lax.axis_index("yh") * 4 + lax.axis_index("x")
    which = jnp.where(block < per_core, core, 1 - core)
    inner = jnp.where(block < per_core, block, block - per_core)
    return (chip * 2 + which) * (params // 2) + inner * depth


def table_kernel(part, width, first, params, words, out):
    depth, wide = out.shape
    row_start = first_parameter(pl.program_id(0) + first, depth, params)
    rows = 32

    def chunk(index, carry):
        start = pl.multiple_of(index * rows, rows)
        cols = columns(0, wide, part, width)
        out[pl.ds(start, rows), :] = signs(words, row_start + start, rows, cols)
        return carry

    lax.fori_loop(0, depth // rows, chunk, 0)


def table(part, width, first, count, depth, params, words):
    return pl.pallas_call(
        functools.partial(table_kernel, part, width, first, params),
        out_shape=jax.ShapeDtypeStruct((count * depth, 8 * width), BF16),
        grid=(count,),
        in_specs=[pl.BlockSpec(memory_space=pltpu.SMEM)],
        out_specs=pl.BlockSpec((depth, 8 * width), lambda k: (k, 0)),
        compiler_params=pltpu.CompilerParams(vmem_limit_bytes=12 << 20),
        cost_estimate=pl.CostEstimate(
            flops=1200 * count * depth * 8 * width,
            bytes_accessed=2 * count * depth * 8 * width,
            transcendentals=0,
        ),
    )(words)


def load_examples(blocks, examples, arrived):
    me = lax.axis_index("zl") * 2 + lax.axis_index("yl")
    half = len(blocks) // 2
    params = blocks[0].shape[1]
    rows = blocks[0].shape[0]
    copies = []
    for index, block in enumerate(blocks):
        kind = index % half
        start = (me ^ min(kind, 3)) * rows + (rows // 2 if kind == 4 else 0)
        target = examples.at[
            pl.ds(pl.multiple_of(start, 32), block.shape[0]),
            (index // half) * params : (index // half + 1) * params,
        ]
        copies.append(pltpu.make_async_copy(block, target, arrived.at[index]))
    for copy in copies:
        copy.start()
    for copy in copies:
        copy.wait()


def write_run(out, total, width):
    for block in range(8):
        out[block] = total[:, block * width : (block + 1) * width] * SCALE


def ready_kernel(split, width, first, second, *refs):
    blocks, (out, examples, total, arrived) = refs[:-4], refs[-4:]
    step = pl.program_id(0)
    depth = first.shape[0]

    @pl.when(step == 0)
    def _():
        load_examples(blocks, examples, arrived)
        total[...] = jnp.zeros_like(total)

    held = examples[:, pl.ds(pl.multiple_of(step * depth, depth), depth)]

    @pl.when(step < split)
    def _():
        total[...] += jnp.dot(held, first[...], preferred_element_type=F32)

    @pl.when(step >= split)
    def _():
        total[...] += jnp.dot(held, second[...], preferred_element_type=F32)

    @pl.when(step == pl.num_programs(0) - 1)
    def _():
        write_run(out, total, width)


def hash_kernel(part, width, words, *refs):
    blocks, (out, examples, total, arrived) = refs[:-4], refs[-4:]
    step = pl.program_id(0)
    params = examples.shape[1]
    depth = params // pl.num_programs(0)
    wide = 512

    @pl.when(step == 0)
    def _():
        load_examples(blocks, examples, arrived)
        total[...] = jnp.zeros_like(total)

    held = examples[:, pl.ds(pl.multiple_of(step * depth, depth), depth)]
    row_start = first_parameter(step, depth, params)
    for first in range(0, 8 * width, wide):
        made = signs(words, row_start, depth, columns(first, wide, part, width))
        total[:, first : first + wide] += jnp.dot(held, made, preferred_element_type=F32)

    @pl.when(step == pl.num_programs(0) - 1)
    def _():
        write_run(out, total, width)


def project(kernel, leading, specs, steps, width, blocks, vmem):
    rows, params = 4 * blocks[0].shape[0], 2 * blocks[0].shape[1]
    return pl.pallas_call(
        kernel,
        out_shape=jax.ShapeDtypeStruct((8, rows, width), F32),
        grid=(steps,),
        in_specs=specs + [pl.BlockSpec(memory_space=pltpu.HBM)] * len(blocks),
        out_specs=pl.BlockSpec((8, rows, width), lambda k: (0, 0, 0)),
        scratch_shapes=[
            pltpu.VMEM((rows, params), BF16),
            pltpu.VMEM((rows, 8 * width), F32),
            pltpu.SemaphoreType.DMA((len(blocks),)),
        ],
        compiler_params=pltpu.CompilerParams(vmem_limit_bytes=vmem << 20),
        cost_estimate=pl.CostEstimate(
            flops=2 * rows * params * 8 * width, bytes_accessed=16 << 20, transcendentals=0
        ),
    )(*leading, *blocks)


def sum_kernel(part, *earlier_and_outs):
    earlier, (whole, keep, send) = earlier_and_outs[:-3], earlier_and_outs[-3:]
    core = lax.axis_index("c")
    width = part.shape[2]
    total = part[0]
    for index in range(1, part.shape[0]):
        total += part[index]
    total = total.astype(BF16)
    for index, value in enumerate(earlier):
        whole[:, index * width : (index + 1) * width] = value[...]
    whole[:, len(earlier) * width :] = total
    mine = slice(len(earlier) * width, (len(earlier) + 1) * width)
    for block in range(2):
        for target, which in ((keep, core), (send, 1 - core)):
            start = pl.multiple_of(block * 128 + which * 64, 64)
            target[block * 64 : (block + 1) * 64, :] = whole[pl.ds(start, 64), mine]


def sum_parts(part, *earlier):
    _, rows, width = part.shape
    shapes = [(rows, width * (1 + len(earlier))), (rows // 2, width), (rows // 2, width)]
    return pl.pallas_call(
        sum_kernel,
        out_shape=[jax.ShapeDtypeStruct(shape, BF16) for shape in shapes],
        compiler_params=pltpu.CompilerParams(vmem_limit_bytes=8 << 20),
    )(part, *earlier)


RING = (0, -1, -2, -3, -4, 1, 2, 3)


def condition_kernel(*refs):
    low, high, (mine, other), (out, pieces, tiles, arrived) = refs[0], refs[1:9], refs[9:11], refs[11:]
    core = lax.axis_index("c")
    yl = lax.axis_index("yl")
    z = lax.axis_index("zh") * 2 + lax.axis_index("zl")
    first = [
        pltpu.make_async_copy(mine, tiles.at[core], arrived.at[16]),
        pltpu.make_async_copy(other, tiles.at[1 - core], arrived.at[17]),
    ]
    copies = []
    for index, away in enumerate(RING):
        for run, source in enumerate((low.at[(z + (away + 8)) & 7], high[index])):
            target = pieces.at[index, :, :, run * 128 : (run + 1) * 128]
            copies.append(pltpu.make_async_copy(source, target, arrived.at[index * 2 + run]))
    for copy in first + copies:
        copy.start()
    out[...] = jnp.zeros_like(out)
    for copy in first:
        copy.wait()
    for index, away in enumerate(RING):
        copies[index * 2].wait()
        copies[index * 2 + 1].wait()
        source = (z + (away + 8)) & 7
        total = None
        for flip in range(4):
            start = pl.multiple_of(((source & 1) * 2 + (core ^ (flip % 2))) * 256, 256)
            tile = tiles[yl ^ (flip // 2), pl.ds(start, 256), :]
            term = jnp.dot(pieces[index, flip], tile, preferred_element_type=F32)
            total = term if total is None else total + term
        out[pl.ds(pl.multiple_of((source >> 1) * 128, 128), 128), :] += total


def condition(low, high, mine, other):
    _, flips, rows, width = low.shape
    return pl.pallas_call(
        condition_kernel,
        out_shape=jax.ShapeDtypeStruct((4 * rows, mine.shape[1]), F32),
        in_specs=[pl.BlockSpec(memory_space=pltpu.HBM)] * 11,
        out_specs=pl.BlockSpec(memory_space=pltpu.VMEM),
        scratch_shapes=[
            pltpu.VMEM((8, flips, rows, 2 * width), BF16),
            pltpu.VMEM((2,) + mine.shape, BF16),
            pltpu.SemaphoreType.DMA((18,)),
        ],
        compiler_params=pltpu.CompilerParams(vmem_limit_bytes=60 << 20),
        cost_estimate=pl.CostEstimate(flops=2 * 512 * 2048 * 1024, bytes_accessed=7 << 20, transcendentals=0),
    )(low, *high, mine, other)


def pair_kernel(parts, near, far, out, rows, pairs):
    core = lax.axis_index("c")
    total = parts[0]
    for index in range(1, parts.shape[0]):
        total += parts[index]
    rows[...] = total.astype(BF16)
    yh = lax.axis_index("yh")
    for flip_yh in range(2):
        for pair_x in range(2):
            value = None
            for zl in range(2):
                for flip in range(2):
                    start = pl.multiple_of((zl * 2 + (core ^ flip)) * 256, 256)
                    term = lax.dot_general(
                        rows[:, pl.ds(start, 256)],
                        (near, far)[flip][pair_x * 2 + zl, flip_yh],
                        (((1,), (1,)), ((), ())),
                        preferred_element_type=F32,
                    )
                    value = term if value is None else value + term
            zh = (yh ^ flip_yh) * 2 + pair_x
            pairs[:, pl.ds(pl.multiple_of(zh * 256, 256), 256)] = value
    for block in range(16):
        piece = pairs[:, block * 64 : (block + 1) * 64]
        out[block, :, :64] = piece[:32]
        out[block, :, 64:] = piece[32:]


def pair(parts, near, far):
    return pl.pallas_call(
        pair_kernel,
        out_shape=jax.ShapeDtypeStruct((16, 32, 128), F32),
        scratch_shapes=[pltpu.VMEM((64, 1024), BF16), pltpu.VMEM((64, 1024), F32)],
        compiler_params=pltpu.CompilerParams(vmem_limit_bytes=12 << 20),
    )(parts, near, far)


def finish_kernel(parts, out):
    total = parts[0]
    for index in range(1, parts.shape[0]):
        total += parts[index]
    total = total * SCALE
    out[:32] = total[:, :64]
    out[32:] = total[:, 64:]


def finish(parts):
    return pl.pallas_call(
        finish_kernel,
        out_shape=jax.ShapeDtypeStruct((64, 64), F32),
    )(parts)


def swap(value, axis):
    return lax.ppermute(value, axis, [(0, 1), (1, 0)])


def step_z(value, by):
    return lax.ppermute(value, ("zh", "zl"), [(i, (i + by) % 8) for i in range(8)])


def ring_and_turn(value, piece, route):
    turned = lax.ppermute(piece, EX + PAR, route)
    up = [step_z(value, 1)]
    down = [step_z(value, 7)]
    up.append(step_z(up[0], 1))
    down.append(step_z(down[0], 7))
    turned, up[1], down[1] = lax.optimization_barrier((turned, up[1], down[1]))
    flipped = swap(turned, "yh")
    up.append(step_z(up[1], 1))
    down.append(step_z(down[1], 7))
    flipped, up[2], down[2] = lax.optimization_barrier((flipped, up[2], down[2]))
    up.append(step_z(up[2], 1))
    return [value] + up + down, jnp.stack([turned, flipped])


def flips(keep, send):
    received = swap(send, "c")
    return jnp.stack([keep, received, swap(keep, "yl"), swap(received, "yl")])


def per_device(gradients, inverse_gram, hash_words):
    half = gradients.shape[0] // 2
    width, depth, params = 128, 1024, 2 * gradients.shape[1]
    split = 5
    words_spec = pl.BlockSpec(memory_space=pltpu.SMEM)
    first = table(0, width, 0, split, depth, params, hash_words)
    second = table(0, width, split, params // depth - split, depth, params, hash_words)

    next_y = swap(gradients, "yl")
    next_z = swap(gradients, "zl")
    first, next_y, next_z = lax.optimization_barrier((first, next_y, next_z))
    own = [gradients, next_y, next_z, swap(next_y[:half], "zl"), swap(next_z[half:], "yl")]
    blocks = own + [swap(a, "c") for a in own]
    other_tile = swap(inverse_gram, "c")

    table_specs = [
        pl.BlockSpec((depth, 8 * width), lambda k: (jnp.minimum(k, split - 1), 0)),
        pl.BlockSpec((depth, 8 * width), lambda k: (jnp.maximum(k - split, 0), 0)),
    ]
    partial = project(
        functools.partial(ready_kernel, split, width), [first, second], table_specs, params // depth, width, blocks, 24
    )
    part = lax.all_to_all(partial, CHIPS, 0, 0, tiled=True)
    partial = project(functools.partial(hash_kernel, 1, width), [hash_words], [words_spec], 16, width, blocks, 60)
    partial, part = lax.optimization_barrier((partial, part))
    next_part = lax.all_to_all(partial, CHIPS, 0, 0, tiled=True)

    route = []
    for z in range(8):
        for yl in range(2):
            for chip in range(8):
                for c in range(2):
                    route.append((((z * 2 + yl) * 8 + chip) * 2 + c, ((chip * 2 + yl) * 8 + z) * 2 + c))
    whole, keep, send = sum_parts(part)
    mine = flips(keep, send)
    low = lax.all_gather(mine, ("zh", "zl"), axis=0)
    next_part, mine = lax.optimization_barrier((next_part, mine))
    whole, keep, send = sum_parts(next_part, whole)
    whole, mine = lax.optimization_barrier((whole, flips(keep, send)))
    high, turned = ring_and_turn(mine, whole, route)
    turned, low = lax.optimization_barrier((turned, low))
    near = lax.all_gather(turned, "x", axis=0)
    far = swap(near, "c")

    conditioned = condition(low, high, inverse_gram, other_tile)
    parts = lax.all_to_all(conditioned.reshape(8, 64, 1024), CHIPS, 0, 0, tiled=True)
    return finish(lax.all_to_all(pair(parts, near, far), EX, 0, 0, tiled=True))


def solution(mesh):
    fine = Mesh(mesh.devices.reshape(4, 2, 2, 2, 4, 2), EX + PAR)
    return jax.shard_map(
        per_device,
        mesh=fine,
        in_specs=(P(EX, PAR), P(PAR, EX), P()),
        out_specs=P(PAR, EX),
        check_vma=False,
    )
```

```python
import functools

import jax
import jax.numpy as jnp
from jax import lax
from jax.experimental import pallas as pl
from jax.experimental.pallas import tpu as pltpu
from jax.sharding import Mesh
from jax.sharding import PartitionSpec as P

FEATURES = 16384
SCALE = FEATURES ** (-0.5)
BF16 = jnp.bfloat16
F32 = jnp.float32

EX = ("zh", "zl", "yl")
CHIPS = ("yh", "x")
PAR = ("yh", "x", "c")
FEATURES_PER_CHIP = FEATURES // 8


def shifted(values, amount):
    return lax.shift_right_logical(values, jnp.full(values.shape, amount, jnp.int32))


def signs(hash_words, row_start, rows, cols):
    m0 = hash_words[0] | 1
    row_ids = lax.broadcasted_iota(jnp.int32, (rows, cols.shape[1]), 0)
    mixed = row_ids * (FEATURES * m0) + (cols * m0 + (row_start * (FEATURES * m0) + hash_words[1]))
    mixed = mixed ^ shifted(mixed, 15)
    mixed = mixed * (hash_words[2] | 1)
    mixed = mixed ^ shifted(mixed, 13)
    mixed = mixed * (hash_words[3] | 1)
    return jnp.where(mixed < 0, BF16(-1), BF16(1))


def columns(first, count, part, width):
    slice_id = lax.axis_index("yl") * 4 + lax.axis_index("zl") * 2 + lax.axis_index("c")
    column = lax.broadcasted_iota(jnp.int32, (1, count), 1)
    group, within = column // width, column % width
    return (group + first // width) * FEATURES_PER_CHIP + within + (slice_id * 256 + part * width)


def first_parameter(block, depth, params):
    per_core = params // 2 // depth
    core = lax.axis_index("c")
    chip = lax.axis_index("yh") * 4 + lax.axis_index("x")
    which = jnp.where(block < per_core, core, 1 - core)
    inner = jnp.where(block < per_core, block, block - per_core)
    return (chip * 2 + which) * (params // 2) + inner * depth


def table_kernel(part, width, first, params, words, out):
    depth, wide = out.shape
    row_start = first_parameter(pl.program_id(0) + first, depth, params)
    rows = 32

    def chunk(index, carry):
        start = pl.multiple_of(index * rows, rows)
        cols = columns(0, wide, part, width)
        out[pl.ds(start, rows), :] = signs(words, row_start + start, rows, cols)
        return carry

    lax.fori_loop(0, depth // rows, chunk, 0)


def table(part, width, first, count, depth, params, words):
    return pl.pallas_call(
        functools.partial(table_kernel, part, width, first, params),
        out_shape=jax.ShapeDtypeStruct((count * depth, 8 * width), BF16),
        grid=(count,),
        in_specs=[pl.BlockSpec(memory_space=pltpu.SMEM)],
        out_specs=pl.BlockSpec((depth, 8 * width), lambda k: (k, 0)),
        compiler_params=pltpu.CompilerParams(vmem_limit_bytes=12 << 20),
        cost_estimate=pl.CostEstimate(
            flops=1200 * count * depth * 8 * width,
            bytes_accessed=2 * count * depth * 8 * width,
            transcendentals=0,
        ),
    )(words)


def load_examples(blocks, examples, arrived):
    me = lax.axis_index("zl") * 2 + lax.axis_index("yl")
    half = len(blocks) // 2
    params = blocks[0].shape[1]
    rows = blocks[0].shape[0]
    copies = []
    for index, block in enumerate(blocks):
        kind = index % half
        start = (me ^ min(kind, 3)) * rows + (rows // 2 if kind == 4 else 0)
        target = examples.at[
            pl.ds(pl.multiple_of(start, 32), block.shape[0]),
            (index // half) * params : (index // half + 1) * params,
        ]
        copies.append(pltpu.make_async_copy(block, target, arrived.at[index]))
    for copy in copies:
        copy.start()
    for copy in copies:
        copy.wait()


def write_run(out, total, width):
    for block in range(8):
        out[block] = total[:, block * width : (block + 1) * width] * SCALE


def ready_kernel(split, width, first, second, *refs):
    blocks, (out, gathered, examples, total, arrived) = refs[:-5], refs[-5:]
    step = pl.program_id(0)
    depth = first.shape[0]
    hand_on = pltpu.make_async_copy(examples, gathered, arrived.at[len(blocks)])

    @pl.when(step == 0)
    def _():
        load_examples(blocks, examples, arrived)
        hand_on.start()
        total[...] = jnp.zeros_like(total)

    held = examples[:, pl.ds(pl.multiple_of(step * depth, depth), depth)]

    @pl.when(step < split)
    def _():
        total[...] += jnp.dot(held, first[...], preferred_element_type=F32)

    @pl.when(step >= split)
    def _():
        total[...] += jnp.dot(held, second[...], preferred_element_type=F32)

    @pl.when(step == pl.num_programs(0) - 1)
    def _():
        hand_on.wait()
        write_run(out, total, width)


def project_ready(first, second, width, blocks):
    rows, params = 4 * blocks[0].shape[0], 2 * blocks[0].shape[1]
    depth = 1024
    split = first.shape[0] // depth
    return pl.pallas_call(
        functools.partial(ready_kernel, split, width),
        out_shape=[
            jax.ShapeDtypeStruct((8, rows, width), F32),
            jax.ShapeDtypeStruct((rows, params), BF16),
        ],
        grid=(params // depth,),
        in_specs=[
            pl.BlockSpec((depth, 8 * width), lambda k: (jnp.minimum(k, split - 1), 0)),
            pl.BlockSpec((depth, 8 * width), lambda k: (jnp.maximum(k - split, 0), 0)),
        ]
        + [pl.BlockSpec(memory_space=pltpu.HBM)] * len(blocks),
        out_specs=[
            pl.BlockSpec((8, rows, width), lambda k: (0, 0, 0)),
            pl.BlockSpec(memory_space=pltpu.HBM),
        ],
        scratch_shapes=[
            pltpu.VMEM((rows, params), BF16),
            pltpu.VMEM((rows, 8 * width), F32),
            pltpu.SemaphoreType.DMA((len(blocks) + 1,)),
        ],
        compiler_params=pltpu.CompilerParams(vmem_limit_bytes=24 << 20),
        cost_estimate=pl.CostEstimate(
            flops=2 * rows * params * 8 * width, bytes_accessed=16 << 20, transcendentals=0
        ),
    )(first, second, *blocks)


def hash_kernel(part, width, words, gathered, out, examples, total, arrived):
    step = pl.program_id(0)
    steps = arrived.shape[0]
    params = examples.shape[1]
    depth = params // steps
    wide = 512

    def bring(index):
        at = pl.ds(pl.multiple_of(index * depth, depth), depth)
        return pltpu.make_async_copy(gathered.at[:, at], examples.at[:, at], arrived.at[index])

    @pl.when(step == 0)
    def _():
        for index in range(steps):
            bring(index).start()
        total[...] = jnp.zeros_like(total)

    bring(step).wait()
    held = examples[:, pl.ds(pl.multiple_of(step * depth, depth), depth)]
    row_start = first_parameter(step, depth, params)
    for first in range(0, 8 * width, wide):
        made = signs(words, row_start, depth, columns(first, wide, part, width))
        total[:, first : first + wide] += jnp.dot(held, made, preferred_element_type=F32)

    @pl.when(step == steps - 1)
    def _():
        write_run(out, total, width)


def project_hash(part, width, words, gathered, steps=16):
    rows, params = gathered.shape
    return pl.pallas_call(
        functools.partial(hash_kernel, part, width),
        out_shape=jax.ShapeDtypeStruct((8, rows, width), F32),
        grid=(steps,),
        in_specs=[pl.BlockSpec(memory_space=pltpu.SMEM), pl.BlockSpec(memory_space=pltpu.HBM)],
        out_specs=pl.BlockSpec((8, rows, width), lambda k: (0, 0, 0)),
        scratch_shapes=[
            pltpu.VMEM((rows, params), BF16),
            pltpu.VMEM((rows, 8 * width), F32),
            pltpu.SemaphoreType.DMA((steps,)),
        ],
        compiler_params=pltpu.CompilerParams(vmem_limit_bytes=60 << 20),
        cost_estimate=pl.CostEstimate(
            flops=2 * rows * params * 8 * width, bytes_accessed=16 << 20, transcendentals=0
        ),
    )(words, gathered)


def sum_kernel(part, whole, keep, send):
    core = lax.axis_index("c")
    total = part[0]
    for index in range(1, part.shape[0]):
        total += part[index]
    whole[...] = total.astype(BF16)
    for block in range(2):
        for target, which in ((keep, core), (send, 1 - core)):
            start = pl.multiple_of(block * 128 + which * 64, 64)
            target[block * 64 : (block + 1) * 64, :] = whole[pl.ds(start, 64), :]


def sum_parts(part):
    _, rows, width = part.shape
    shapes = [(rows, width), (rows // 2, width), (rows // 2, width)]
    return pl.pallas_call(
        sum_kernel,
        out_shape=[jax.ShapeDtypeStruct(shape, BF16) for shape in shapes],
        compiler_params=pltpu.CompilerParams(vmem_limit_bytes=8 << 20),
    )(part)


RING = (0, -1, -2, -3, -4, 1, 2, 3)


def condition_kernel(*refs):
    low, high, (mine, other), (out, pieces, tiles, arrived) = refs[0], refs[1:9], refs[9:11], refs[11:]
    core = lax.axis_index("c")
    yl = lax.axis_index("yl")
    z = lax.axis_index("zh") * 2 + lax.axis_index("zl")
    zl = lax.axis_index("zl")
    tile_copies = []
    for group in range(2):
        rows = pl.ds(pl.multiple_of((zl ^ group) * 512, 512), 512)
        for which, (source, place) in enumerate(((mine, core), (other, 1 - core))):
            tile_copies.append(
                pltpu.make_async_copy(
                    source.at[rows, :], tiles.at[place, rows, :], arrived.at[16 + group * 2 + which]
                )
            )
    copies = []
    for index, away in enumerate(RING):
        for run, source in enumerate((low.at[(z + (away + 8)) & 7], high[index])):
            target = pieces.at[index, :, :, run * 128 : (run + 1) * 128]
            copies.append(pltpu.make_async_copy(source, target, arrived.at[index * 2 + run]))
    for group in range(2):
        for copy in tile_copies[group * 2 : group * 2 + 2]:
            copy.start()
        for index, away in enumerate(RING):
            if away % 2 == group:
                copies[index * 2].start()
                copies[index * 2 + 1].start()
    for group in range(2):
        for copy in tile_copies[group * 2 : group * 2 + 2]:
            copy.wait()
        for index, away in enumerate(RING):
            if away % 2 != group:
                continue
            copies[index * 2].wait()
            copies[index * 2 + 1].wait()
            source = (z + (away + 8)) & 7
            total = None
            for flip in range(4):
                start = pl.multiple_of(((zl ^ group) * 2 + (core ^ (flip % 2))) * 256, 256)
                tile = tiles[yl ^ (flip // 2), pl.ds(start, 256), :]
                term = jnp.dot(pieces[index, flip], tile, preferred_element_type=F32)
                total = term if total is None else total + term
            at = pl.ds(pl.multiple_of((source >> 1) * 128, 128), 128)
            if group == 0:
                out[at, :] = total
            else:
                out[at, :] += total


def condition(low, high, mine, other):
    _, flips, rows, width = low.shape
    return pl.pallas_call(
        condition_kernel,
        out_shape=jax.ShapeDtypeStruct((4 * rows, mine.shape[1]), F32),
        in_specs=[pl.BlockSpec(memory_space=pltpu.HBM)] * 11,
        out_specs=pl.BlockSpec(memory_space=pltpu.VMEM),
        scratch_shapes=[
            pltpu.VMEM((8, flips, rows, 2 * width), BF16),
            pltpu.VMEM((2,) + mine.shape, BF16),
            pltpu.SemaphoreType.DMA((20,)),
        ],
        compiler_params=pltpu.CompilerParams(vmem_limit_bytes=60 << 20),
        cost_estimate=pl.CostEstimate(flops=2 * 512 * 2048 * 1024, bytes_accessed=7 << 20, transcendentals=0),
    )(low, *high, mine, other)


def pair_kernel(parts, *refs):
    features, (out, rows, pairs) = refs[:8], refs[8:]
    yh, x, core = (lax.axis_index(name) for name in PAR)
    total = parts[0]
    for index in range(1, parts.shape[0]):
        total += parts[index]
    rows[...] = total.astype(BF16)
    pairs[...] = jnp.zeros_like(pairs)
    for flip_yh in range(2):
        for shift in range(4):
            place = (x + 4 - shift) & 3
            zh = (yh ^ flip_yh) * 2 + (place >> 1)
            value = None
            for flip_core in range(2):
                start = pl.multiple_of(((place & 1) * 2 + (core ^ flip_core)) * 256, 256)
                held = features[flip_core * 4 + shift]
                term = lax.dot_general(
                    rows[:, pl.ds(start, 256)],
                    jnp.concatenate([held[flip_yh * 2], held[flip_yh * 2 + 1]], axis=1),
                    (((1,), (1,)), ((), ())),
                    preferred_element_type=F32,
                )
                value = term if value is None else value + term
            pairs[:, pl.ds(pl.multiple_of(zh * 256, 256), 256)] += value
    for block in range(16):
        piece = pairs[:, block * 64 : (block + 1) * 64]
        out[block % 4, block // 4, :, :64] = piece[:32]
        out[block % 4, block // 4, :, 64:] = piece[32:]


def pair(parts, features):
    return pl.pallas_call(
        pair_kernel,
        out_shape=jax.ShapeDtypeStruct((4, 4, 32, 128), F32),
        scratch_shapes=[pltpu.VMEM((64, 1024), BF16), pltpu.VMEM((64, 1024), F32)],
        compiler_params=pltpu.CompilerParams(vmem_limit_bytes=12 << 20),
    )(parts, *features)


def add_kernel(parts, out):
    out[...] = (parts[0] + parts[1]) + (parts[2] + parts[3])


def add(parts):
    return pl.pallas_call(add_kernel, out_shape=jax.ShapeDtypeStruct(parts.shape[1:], F32))(parts)


def finish_kernel(parts, out):
    total = ((parts[0] + parts[1]) + (parts[2] + parts[3])) * SCALE
    out[:32] = total[:, :64]
    out[32:] = total[:, 64:]


def finish(parts):
    return pl.pallas_call(finish_kernel, out_shape=jax.ShapeDtypeStruct((64, 64), F32))(parts)


def swap(value, axis):
    return lax.ppermute(value, axis, [(0, 1), (1, 0)])


def step_z(value, by):
    return lax.ppermute(value, ("zh", "zl"), [(i, (i + by) % 8) for i in range(8)])


def ring_and_turn(value, earlier, piece, route):
    turned = lax.ppermute(piece, EX + PAR, route)
    up = [step_z(value, 1)]
    down = [step_z(value, 7)]
    up.append(step_z(up[0], 1))
    down.append(step_z(down[0], 7))
    turned, up[1], down[1] = lax.optimization_barrier((turned, up[1], down[1]))
    both = jnp.stack([earlier, turned])
    flipped = swap(both, "yh")
    up.append(step_z(up[1], 1))
    down.append(step_z(down[1], 7))
    flipped, up[2], down[2] = lax.optimization_barrier((flipped, up[2], down[2]))
    up.append(step_z(up[2], 1))
    four = jnp.concatenate([both, flipped])
    along_x = [four]
    for by in range(1, 4):
        along_x.append(lax.ppermute(four, "x", [(i, (i + by) % 4) for i in range(4)]))
    return [value] + up + down, along_x


def flips(keep, send):
    received = swap(send, "c")
    return jnp.stack([keep, received, swap(keep, "yl"), swap(received, "yl")])


def per_device(gradients, inverse_gram, hash_words):
    half = gradients.shape[0] // 2
    width, depth, params = 128, 1024, 2 * gradients.shape[1]
    split = 5
    first = table(0, width, 0, split, depth, params, hash_words)
    second = table(0, width, split, params // depth - split, depth, params, hash_words)

    next_y = swap(gradients, "yl")
    next_z = swap(gradients, "zl")
    first, next_y, next_z = lax.optimization_barrier((first, next_y, next_z))
    diag_a, diag_b = swap(next_y[:half], "zl"), swap(next_z[half:], "yl")
    diag_a, diag_b, second = lax.optimization_barrier((diag_a, diag_b, second))
    own = [gradients, next_y, next_z, diag_a, diag_b]
    blocks = own + [swap(a, "c") for a in own]
    other_tile = swap(inverse_gram, "c")

    partial, gathered = project_ready(first, second, width, blocks)
    part = lax.all_to_all(partial, CHIPS, 0, 0, tiled=True)
    partial = project_hash(1, width, hash_words, gathered)
    partial, part = lax.optimization_barrier((partial, part))
    next_part = lax.all_to_all(partial, CHIPS, 0, 0, tiled=True)

    route = []
    for z in range(8):
        for yl in range(2):
            for chip in range(8):
                for c in range(2):
                    route.append((((z * 2 + yl) * 8 + chip) * 2 + c, ((chip * 2 + yl) * 8 + z) * 2 + c))
    whole, keep, send = sum_parts(part)
    mine = flips(keep, send)
    low = lax.all_gather(mine, ("zh", "zl"), axis=0)
    turned = lax.ppermute(whole, EX + PAR, route)
    next_part, mine, turned = lax.optimization_barrier((next_part, mine, turned))
    whole, keep, send = sum_parts(next_part)
    whole, mine = lax.optimization_barrier((whole, flips(keep, send)))
    high, near = ring_and_turn(mine, turned, whole, route)

    conditioned = condition(low, high, inverse_gram, other_tile)
    conditioned, near = lax.optimization_barrier((conditioned, near))
    far = [swap(v, "c") for v in near]
    parts = lax.all_to_all(conditioned.reshape(8, 64, 1024), CHIPS, 0, 0, tiled=True)
    scores = add(lax.all_to_all(pair(parts, near + far), ("zl", "yl"), 0, 0, tiled=True))
    return finish(lax.all_to_all(scores, "zh", 0, 0, tiled=True))


def solution(mesh):
    fine = Mesh(mesh.devices.reshape(4, 2, 2, 2, 4, 2), EX + PAR)
    return jax.shard_map(
        per_device,
        mesh=fine,
        in_specs=(P(EX, PAR), P(PAR, EX), P()),
        out_specs=P(PAR, EX),
        check_vma=False,
    )
```

```python
import functools

import jax
import jax.numpy as jnp
from jax import lax
from jax.experimental import pallas as pl
from jax.experimental.pallas import tpu as pltpu
from jax.sharding import Mesh
from jax.sharding import PartitionSpec as P

FEATURES = 16384
SCALE = FEATURES ** (-0.5)
BF16 = jnp.bfloat16
F32 = jnp.float32

EX = ("zh", "zl", "yl")
CHIPS = ("yh", "x")
PAR = ("yh", "x", "c")
FEATURES_PER_CHIP = FEATURES // 8


def shifted(values, amount):
    return lax.shift_right_logical(values, jnp.full(values.shape, amount, jnp.int32))


def signs(hash_words, row_start, rows, cols):
    m0 = hash_words[0] | 1
    row_ids = lax.broadcasted_iota(jnp.int32, (rows, cols.shape[1]), 0)
    mixed = row_ids * (FEATURES * m0) + (cols * m0 + (row_start * (FEATURES * m0) + hash_words[1]))
    mixed = mixed ^ shifted(mixed, 15)
    mixed = mixed * (hash_words[2] | 1)
    mixed = mixed ^ shifted(mixed, 13)
    mixed = mixed * (hash_words[3] | 1)
    return jnp.where(mixed < 0, BF16(-1), BF16(1))


def columns(first, count, part, width):
    slice_id = lax.axis_index("yl") * 4 + lax.axis_index("zl") * 2 + lax.axis_index("c")
    column = lax.broadcasted_iota(jnp.int32, (1, count), 1)
    group, within = column // width, column % width
    return (group + first // width) * FEATURES_PER_CHIP + within + (slice_id * 256 + part * width)


def first_parameter(block, depth, params):
    per_core = params // 2 // depth
    core = lax.axis_index("c")
    chip = lax.axis_index("yh") * 4 + lax.axis_index("x")
    which = jnp.where(block < per_core, core, 1 - core)
    inner = jnp.where(block < per_core, block, block - per_core)
    return (chip * 2 + which) * (params // 2) + inner * depth


def table_kernel(part, width, first, params, words, out):
    depth, wide = out.shape
    row_start = first_parameter(pl.program_id(0) + first, depth, params)
    rows = 32

    def chunk(index, carry):
        start = pl.multiple_of(index * rows, rows)
        cols = columns(0, wide, part, width)
        out[pl.ds(start, rows), :] = signs(words, row_start + start, rows, cols)
        return carry

    lax.fori_loop(0, depth // rows, chunk, 0)


def table(part, width, first, count, depth, params, words):
    return pl.pallas_call(
        functools.partial(table_kernel, part, width, first, params),
        out_shape=jax.ShapeDtypeStruct((count * depth, 8 * width), BF16),
        grid=(count,),
        in_specs=[pl.BlockSpec(memory_space=pltpu.SMEM)],
        out_specs=pl.BlockSpec((depth, 8 * width), lambda k: (k, 0)),
        compiler_params=pltpu.CompilerParams(vmem_limit_bytes=12 << 20),
        cost_estimate=pl.CostEstimate(
            flops=1200 * count * depth * 8 * width,
            bytes_accessed=2 * count * depth * 8 * width,
            transcendentals=0,
        ),
    )(words)


def load_examples(blocks, examples, arrived):
    me = lax.axis_index("zl") * 2 + lax.axis_index("yl")
    half = len(blocks) // 2
    params = blocks[0].shape[1]
    rows = blocks[0].shape[0]
    copies = []
    for index, block in enumerate(blocks):
        kind = index % half
        start = (me ^ min(kind, 3)) * rows + (rows // 2 if kind == 4 else 0)
        target = examples.at[
            pl.ds(pl.multiple_of(start, 32), block.shape[0]),
            (index // half) * params : (index // half + 1) * params,
        ]
        copies.append(pltpu.make_async_copy(block, target, arrived.at[index]))
    for copy in copies:
        copy.start()
    for copy in copies:
        copy.wait()


def write_run(out, total, width):
    for block in range(8):
        out[block] = total[:, block * width : (block + 1) * width] * SCALE


def ready_kernel(split, width, first, second, *refs):
    blocks, (out, gathered, examples, total, arrived) = refs[:-5], refs[-5:]
    step = pl.program_id(0)
    depth = first.shape[0]
    hand_on = pltpu.make_async_copy(examples, gathered, arrived.at[len(blocks)])

    @pl.when(step == 0)
    def _():
        load_examples(blocks, examples, arrived)
        hand_on.start()
        total[...] = jnp.zeros_like(total)

    held = examples[:, pl.ds(pl.multiple_of(step * depth, depth), depth)]

    @pl.when(step < split)
    def _():
        total[...] += jnp.dot(held, first[...], preferred_element_type=F32)

    @pl.when(step >= split)
    def _():
        total[...] += jnp.dot(held, second[...], preferred_element_type=F32)

    @pl.when(step == pl.num_programs(0) - 1)
    def _():
        hand_on.wait()
        write_run(out, total, width)


def project_ready(first, second, width, blocks):
    rows, params = 4 * blocks[0].shape[0], 2 * blocks[0].shape[1]
    depth = 1024
    split = first.shape[0] // depth
    return pl.pallas_call(
        functools.partial(ready_kernel, split, width),
        out_shape=[
            jax.ShapeDtypeStruct((8, rows, width), F32),
            jax.ShapeDtypeStruct((rows, params), BF16),
        ],
        grid=(params // depth,),
        in_specs=[
            pl.BlockSpec((depth, 8 * width), lambda k: (jnp.minimum(k, split - 1), 0)),
            pl.BlockSpec((depth, 8 * width), lambda k: (jnp.maximum(k - split, 0), 0)),
        ]
        + [pl.BlockSpec(memory_space=pltpu.HBM)] * len(blocks),
        out_specs=[
            pl.BlockSpec((8, rows, width), lambda k: (0, 0, 0)),
            pl.BlockSpec(memory_space=pltpu.HBM),
        ],
        scratch_shapes=[
            pltpu.VMEM((rows, params), BF16),
            pltpu.VMEM((rows, 8 * width), F32),
            pltpu.SemaphoreType.DMA((len(blocks) + 1,)),
        ],
        compiler_params=pltpu.CompilerParams(vmem_limit_bytes=24 << 20),
        cost_estimate=pl.CostEstimate(
            flops=2 * rows * params * 8 * width, bytes_accessed=16 << 20, transcendentals=0
        ),
    )(first, second, *blocks)


def hash_kernel(part, width, words, gathered, out, examples, total, arrived):
    step = pl.program_id(0)
    steps = arrived.shape[0]
    params = examples.shape[1]
    depth = params // steps
    wide = 512

    def bring(index):
        at = pl.ds(pl.multiple_of(index * depth, depth), depth)
        return pltpu.make_async_copy(gathered.at[:, at], examples.at[:, at], arrived.at[index])

    @pl.when(step == 0)
    def _():
        for index in range(steps):
            bring(index).start()
        total[...] = jnp.zeros_like(total)

    bring(step).wait()
    held = examples[:, pl.ds(pl.multiple_of(step * depth, depth), depth)]
    row_start = first_parameter(step, depth, params)
    for first in range(0, 8 * width, wide):
        made = signs(words, row_start, depth, columns(first, wide, part, width))
        total[:, first : first + wide] += jnp.dot(held, made, preferred_element_type=F32)

    @pl.when(step == steps - 1)
    def _():
        write_run(out, total, width)


def project_hash(part, width, words, gathered, steps=16):
    rows, params = gathered.shape
    return pl.pallas_call(
        functools.partial(hash_kernel, part, width),
        out_shape=jax.ShapeDtypeStruct((8, rows, width), F32),
        grid=(steps,),
        in_specs=[pl.BlockSpec(memory_space=pltpu.SMEM), pl.BlockSpec(memory_space=pltpu.HBM)],
        out_specs=pl.BlockSpec((8, rows, width), lambda k: (0, 0, 0)),
        scratch_shapes=[
            pltpu.VMEM((rows, params), BF16),
            pltpu.VMEM((rows, 8 * width), F32),
            pltpu.SemaphoreType.DMA((steps,)),
        ],
        compiler_params=pltpu.CompilerParams(vmem_limit_bytes=60 << 20),
        cost_estimate=pl.CostEstimate(
            flops=2 * rows * params * 8 * width, bytes_accessed=16 << 20, transcendentals=0
        ),
    )(words, gathered)


def sum_kernel(part, whole, keep, send):
    core = lax.axis_index("c")
    total = part[0]
    for index in range(1, part.shape[0]):
        total += part[index]
    whole[...] = total.astype(BF16)
    for block in range(2):
        for target, which in ((keep, core), (send, 1 - core)):
            start = pl.multiple_of(block * 128 + which * 64, 64)
            target[block * 64 : (block + 1) * 64, :] = whole[pl.ds(start, 64), :]


def sum_parts(part):
    _, rows, width = part.shape
    shapes = [(rows, width), (rows // 2, width), (rows // 2, width)]
    return pl.pallas_call(
        sum_kernel,
        out_shape=[jax.ShapeDtypeStruct(shape, BF16) for shape in shapes],
        compiler_params=pltpu.CompilerParams(vmem_limit_bytes=8 << 20),
    )(part)


RING = (0, -1, -2, -3, -4, 1, 2, 3)


def condition_kernel(*refs):
    low, high, (mine, other), (out, pieces, tiles, arrived) = refs[0], refs[1:9], refs[9:11], refs[11:]
    core = lax.axis_index("c")
    yl = lax.axis_index("yl")
    z = lax.axis_index("zh") * 2 + lax.axis_index("zl")
    zl = lax.axis_index("zl")
    tile_copies = []
    for group in range(2):
        rows = pl.ds(pl.multiple_of((zl ^ group) * 512, 512), 512)
        for which, (source, place) in enumerate(((mine, core), (other, 1 - core))):
            tile_copies.append(
                pltpu.make_async_copy(
                    source.at[rows, :], tiles.at[place, rows, :], arrived.at[16 + group * 2 + which]
                )
            )
    copies = []
    for index, away in enumerate(RING):
        for run, source in enumerate((low.at[(z + (away + 8)) & 7], high[index])):
            target = pieces.at[index, :, :, run * 128 : (run + 1) * 128]
            copies.append(pltpu.make_async_copy(source, target, arrived.at[index * 2 + run]))
    for group in range(2):
        for copy in tile_copies[group * 2 : group * 2 + 2]:
            copy.start()
        for index, away in enumerate(RING):
            if away % 2 == group:
                copies[index * 2].start()
                copies[index * 2 + 1].start()
    for group in range(2):
        for copy in tile_copies[group * 2 : group * 2 + 2]:
            copy.wait()
        for index, away in enumerate(RING):
            if away % 2 != group:
                continue
            copies[index * 2].wait()
            copies[index * 2 + 1].wait()
            source = (z + (away + 8)) & 7
            total = None
            for flip in range(4):
                start = pl.multiple_of(((zl ^ group) * 2 + (core ^ (flip % 2))) * 256, 256)
                tile = tiles[yl ^ (flip // 2), pl.ds(start, 256), :]
                term = jnp.dot(pieces[index, flip], tile, preferred_element_type=F32)
                total = term if total is None else total + term
            at = pl.ds(pl.multiple_of((source >> 1) * 128, 128), 128)
            if group == 0:
                out[at, :] = total
            else:
                out[at, :] += total


def condition(low, high, mine, other):
    _, flips, rows, width = low.shape
    return pl.pallas_call(
        condition_kernel,
        out_shape=jax.ShapeDtypeStruct((4 * rows, mine.shape[1]), F32),
        in_specs=[pl.BlockSpec(memory_space=pltpu.HBM)] * 11,
        out_specs=pl.BlockSpec(memory_space=pltpu.VMEM),
        scratch_shapes=[
            pltpu.VMEM((8, flips, rows, 2 * width), BF16),
            pltpu.VMEM((2,) + mine.shape, BF16),
            pltpu.SemaphoreType.DMA((20,)),
        ],
        compiler_params=pltpu.CompilerParams(vmem_limit_bytes=60 << 20),
        cost_estimate=pl.CostEstimate(flops=2 * 512 * 2048 * 1024, bytes_accessed=7 << 20, transcendentals=0),
    )(low, *high, mine, other)


def join_kernel(*refs):
    for index, ref in enumerate(refs[:-1]):
        refs[-1][index] = ref[...]


def join(values):
    return pl.pallas_call(
        join_kernel,
        out_shape=jax.ShapeDtypeStruct((len(values),) + values[0].shape, values[0].dtype),
        compiler_params=pltpu.CompilerParams(vmem_limit_bytes=6 << 20),
    )(*values)


def pair_kernel(parts, *refs):
    features, (out, rows, pairs) = refs[:2], refs[2:]
    yh, x, core = (lax.axis_index(name) for name in PAR)
    total = parts[0]
    for index in range(1, parts.shape[0]):
        total += parts[index]
    rows[...] = total.astype(BF16)
    pairs[...] = jnp.zeros_like(pairs)
    for flip_yh in range(2):
        for shift in range(4):
            place = (x + 4 - shift) & 3
            zh = (yh ^ flip_yh) * 2 + (place >> 1)
            value = None
            for flip_core in range(2):
                start = pl.multiple_of(((place & 1) * 2 + (core ^ flip_core)) * 256, 256)
                held = features[flip_core].at[shift, flip_yh]
                term = lax.dot_general(
                    rows[:, pl.ds(start, 256)],
                    jnp.concatenate([held[0], held[1]], axis=1),
                    (((1,), (1,)), ((), ())),
                    preferred_element_type=F32,
                )
                value = term if value is None else value + term
            pairs[:, pl.ds(pl.multiple_of(zh * 256, 256), 256)] += value
    for block in range(16):
        piece = pairs[:, block * 64 : (block + 1) * 64]
        out[block, :, :64] = piece[:32]
        out[block, :, 64:] = piece[32:]


def pair(parts, near, far):
    return pl.pallas_call(
        pair_kernel,
        out_shape=jax.ShapeDtypeStruct((16, 32, 128), F32),
        scratch_shapes=[pltpu.VMEM((64, 1024), BF16), pltpu.VMEM((64, 1024), F32)],
        compiler_params=pltpu.CompilerParams(vmem_limit_bytes=12 << 20),
    )(parts, near, far)


def finish_kernel(parts, out):
    total = parts[0]
    for index in range(1, parts.shape[0]):
        total += parts[index]
    total = total * SCALE
    out[:32] = total[:, :64]
    out[32:] = total[:, 64:]


def finish(parts):
    return pl.pallas_call(finish_kernel, out_shape=jax.ShapeDtypeStruct((64, 64), F32))(parts)


def swap(value, axis):
    return lax.ppermute(value, axis, [(0, 1), (1, 0)])


def step_z(value, by):
    return lax.ppermute(value, ("zh", "zl"), [(i, (i + by) % 8) for i in range(8)])


def ring(value):
    up = [step_z(value, 1)]
    down = [step_z(value, 7)]
    for _ in range(2):
        up.append(step_z(up[-1], 1))
        down.append(step_z(down[-1], 7))
    up.append(step_z(up[-1], 1))
    return [value] + up + down


def flips(keep, send):
    received = swap(send, "c")
    return join([keep, received, swap(keep, "yl"), swap(received, "yl")])


def per_device(gradients, inverse_gram, hash_words):
    half = gradients.shape[0] // 2
    width, depth, params = 128, 1024, 2 * gradients.shape[1]
    split = 5
    first = table(0, width, 0, split, depth, params, hash_words)
    second = table(0, width, split, params // depth - split, depth, params, hash_words)

    next_y = swap(gradients, "yl")
    next_z = swap(gradients, "zl")
    first, next_y, next_z = lax.optimization_barrier((first, next_y, next_z))
    diag_a, diag_b = swap(next_y[:half], "zl"), swap(next_z[half:], "yl")
    diag_a, diag_b, second = lax.optimization_barrier((diag_a, diag_b, second))
    own = [gradients, next_y, next_z, diag_a, diag_b]
    blocks = own + [swap(a, "c") for a in own]
    other_tile = swap(inverse_gram, "c")

    partial, gathered = project_ready(first, second, width, blocks)
    part = lax.all_to_all(partial, CHIPS, 0, 0, tiled=True)
    partial = project_hash(1, width, hash_words, gathered)
    partial, part = lax.optimization_barrier((partial, part))
    next_part = lax.all_to_all(partial, CHIPS, 0, 0, tiled=True)

    route = []
    for z in range(8):
        for yl in range(2):
            for chip in range(8):
                for c in range(2):
                    route.append((((z * 2 + yl) * 8 + chip) * 2 + c, ((chip * 2 + yl) * 8 + z) * 2 + c))
    whole, keep, send = sum_parts(part)
    mine = flips(keep, send)
    low = lax.all_gather(mine, ("zh", "zl"), axis=0)
    turned = lax.ppermute(whole, EX + PAR, route)
    next_part, mine, turned = lax.optimization_barrier((next_part, mine, turned))
    whole, keep, send = sum_parts(next_part)
    whole, mine = lax.optimization_barrier((whole, flips(keep, send)))
    whole, high = lax.optimization_barrier((whole, ring(mine)))
    next_turned = lax.ppermute(whole, EX + PAR, route)
    conditioned = condition(low, high, inverse_gram, other_tile)
    conditioned, next_turned = lax.optimization_barrier((conditioned, next_turned))
    parts = lax.all_to_all(conditioned.reshape(8, 64, 1024), CHIPS, 0, 0, tiled=True)

    both = join([turned, next_turned])
    four = join([both, swap(both, "yh")])
    near = [four]
    for by in range(1, 4):
        near.append(lax.ppermute(four, "x", [(i, (i + by) % 4) for i in range(4)]))
    near = join(near)
    return finish(lax.all_to_all(pair(parts, near, swap(near, "c")), EX, 0, 0, tiled=True))


def solution(mesh):
    fine = Mesh(mesh.devices.reshape(4, 2, 2, 2, 4, 2), EX + PAR)
    return jax.shard_map(
        per_device,
        mesh=fine,
        in_specs=(P(EX, PAR), P(PAR, EX), P()),
        out_specs=P(PAR, EX),
        check_vma=False,
    )
```

```python
import functools

import jax
import jax.numpy as jnp
from jax import lax
from jax.experimental import pallas as pl
from jax.experimental.pallas import tpu as pltpu
from jax.sharding import Mesh
from jax.sharding import PartitionSpec as P

FEATURES = 16384
SCALE = FEATURES ** (-0.5)
BF16 = jnp.bfloat16
F32 = jnp.float32

EX = ("zh", "zl", "yl")
CHIPS = ("yh", "x")
PAR = ("yh", "x", "c")
FEATURES_PER_CHIP = FEATURES // 8


def shifted(values, amount):
    return lax.shift_right_logical(values, jnp.full(values.shape, amount, jnp.int32))


def signs(hash_words, row_start, rows, cols):
    m0 = hash_words[0] | 1
    row_ids = lax.broadcasted_iota(jnp.int32, (rows, cols.shape[1]), 0)
    mixed = row_ids * (FEATURES * m0) + (cols * m0 + (row_start * (FEATURES * m0) + hash_words[1]))
    mixed = mixed ^ shifted(mixed, 15)
    mixed = mixed * (hash_words[2] | 1)
    mixed = mixed ^ shifted(mixed, 13)
    mixed = mixed * (hash_words[3] | 1)
    return jnp.where(mixed < 0, BF16(-1), BF16(1))


def columns(first, count, part, width):
    slice_id = lax.axis_index("yl") * 4 + lax.axis_index("zl") * 2 + lax.axis_index("c")
    column = lax.broadcasted_iota(jnp.int32, (1, count), 1)
    group, within = column // width, column % width
    return (group + first // width) * FEATURES_PER_CHIP + within + (slice_id * 256 + part * width)


def first_parameter(block, depth, params):
    per_core = params // 2 // depth
    core = lax.axis_index("c")
    chip = lax.axis_index("yh") * 4 + lax.axis_index("x")
    which = jnp.where(block < per_core, core, 1 - core)
    inner = jnp.where(block < per_core, block, block - per_core)
    return (chip * 2 + which) * (params // 2) + inner * depth


def table_kernel(part, width, first, params, words, out):
    depth, wide = out.shape
    row_start = first_parameter(pl.program_id(0) + first, depth, params)
    rows = 32

    def chunk(index, carry):
        start = pl.multiple_of(index * rows, rows)
        cols = columns(0, wide, part, width)
        out[pl.ds(start, rows), :] = signs(words, row_start + start, rows, cols)
        return carry

    lax.fori_loop(0, depth // rows, chunk, 0)


def table(part, width, first, count, depth, params, words):
    return pl.pallas_call(
        functools.partial(table_kernel, part, width, first, params),
        out_shape=jax.ShapeDtypeStruct((count * depth, 8 * width), BF16),
        grid=(count,),
        in_specs=[pl.BlockSpec(memory_space=pltpu.SMEM)],
        out_specs=pl.BlockSpec((depth, 8 * width), lambda k: (k, 0)),
        compiler_params=pltpu.CompilerParams(vmem_limit_bytes=12 << 20),
        cost_estimate=pl.CostEstimate(
            flops=1200 * count * depth * 8 * width,
            bytes_accessed=2 * count * depth * 8 * width,
            transcendentals=0,
        ),
    )(words)


def load_examples(blocks, examples, arrived):
    me = lax.axis_index("zl") * 2 + lax.axis_index("yl")
    half = len(blocks) // 2
    params = blocks[0].shape[1]
    rows = blocks[0].shape[0]
    copies = []
    for index, block in enumerate(blocks):
        kind = index % half
        start = (me ^ min(kind, 3)) * rows + (rows // 2 if kind == 4 else 0)
        target = examples.at[
            pl.ds(pl.multiple_of(start, 32), block.shape[0]),
            (index // half) * params : (index // half + 1) * params,
        ]
        copies.append(pltpu.make_async_copy(block, target, arrived.at[index]))
    for copy in copies:
        copy.start()
    for copy in copies:
        copy.wait()


def write_run(out, total, width):
    for block in range(8):
        out[block] = total[:, block * width : (block + 1) * width] * SCALE


def ready_kernel(split, width, first, second, *refs):
    blocks, (out, gathered, examples, total, arrived) = refs[:-5], refs[-5:]
    step = pl.program_id(0)
    depth = first.shape[0]
    hand_on = pltpu.make_async_copy(examples, gathered, arrived.at[len(blocks)])

    @pl.when(step == 0)
    def _():
        load_examples(blocks, examples, arrived)
        hand_on.start()
        total[...] = jnp.zeros_like(total)

    held = examples[:, pl.ds(pl.multiple_of(step * depth, depth), depth)]

    @pl.when(step < split)
    def _():
        total[...] += jnp.dot(held, first[...], preferred_element_type=F32)

    @pl.when(step >= split)
    def _():
        total[...] += jnp.dot(held, second[...], preferred_element_type=F32)

    @pl.when(step == pl.num_programs(0) - 1)
    def _():
        hand_on.wait()
        write_run(out, total, width)


def project_ready(first, second, width, blocks):
    rows, params = 4 * blocks[0].shape[0], 2 * blocks[0].shape[1]
    depth = 1024
    split = first.shape[0] // depth
    return pl.pallas_call(
        functools.partial(ready_kernel, split, width),
        out_shape=[
            jax.ShapeDtypeStruct((8, rows, width), F32),
            jax.ShapeDtypeStruct((rows, params), BF16),
        ],
        grid=(params // depth,),
        in_specs=[
            pl.BlockSpec((depth, 8 * width), lambda k: (jnp.minimum(k, split - 1), 0)),
            pl.BlockSpec((depth, 8 * width), lambda k: (jnp.maximum(k - split, 0), 0)),
        ]
        + [pl.BlockSpec(memory_space=pltpu.HBM)] * len(blocks),
        out_specs=[
            pl.BlockSpec((8, rows, width), lambda k: (0, 0, 0)),
            pl.BlockSpec(memory_space=pltpu.HBM),
        ],
        scratch_shapes=[
            pltpu.VMEM((rows, params), BF16),
            pltpu.VMEM((rows, 8 * width), F32),
            pltpu.SemaphoreType.DMA((len(blocks) + 1,)),
        ],
        compiler_params=pltpu.CompilerParams(vmem_limit_bytes=24 << 20),
        cost_estimate=pl.CostEstimate(
            flops=2 * rows * params * 8 * width, bytes_accessed=16 << 20, transcendentals=0
        ),
    )(first, second, *blocks)


def hash_kernel(part, width, words, gathered, out, examples, total, arrived):
    step = pl.program_id(0)
    steps = arrived.shape[0]
    params = examples.shape[1]
    depth = params // steps
    wide = 512

    def bring(index):
        at = pl.ds(pl.multiple_of(index * depth, depth), depth)
        return pltpu.make_async_copy(gathered.at[:, at], examples.at[:, at], arrived.at[index])

    @pl.when(step == 0)
    def _():
        for index in range(steps):
            bring(index).start()
        total[...] = jnp.zeros_like(total)

    bring(step).wait()
    held = examples[:, pl.ds(pl.multiple_of(step * depth, depth), depth)]
    row_start = first_parameter(step, depth, params)
    for first in range(0, 8 * width, wide):
        made = signs(words, row_start, depth, columns(first, wide, part, width))
        total[:, first : first + wide] += jnp.dot(held, made, preferred_element_type=F32)

    @pl.when(step == steps - 1)
    def _():
        write_run(out, total, width)


def project_hash(part, width, words, gathered, steps=16):
    rows, params = gathered.shape
    return pl.pallas_call(
        functools.partial(hash_kernel, part, width),
        out_shape=jax.ShapeDtypeStruct((8, rows, width), F32),
        grid=(steps,),
        in_specs=[pl.BlockSpec(memory_space=pltpu.SMEM), pl.BlockSpec(memory_space=pltpu.HBM)],
        out_specs=pl.BlockSpec((8, rows, width), lambda k: (0, 0, 0)),
        scratch_shapes=[
            pltpu.VMEM((rows, params), BF16),
            pltpu.VMEM((rows, 8 * width), F32),
            pltpu.SemaphoreType.DMA((steps,)),
        ],
        compiler_params=pltpu.CompilerParams(vmem_limit_bytes=60 << 20),
        cost_estimate=pl.CostEstimate(
            flops=2 * rows * params * 8 * width, bytes_accessed=16 << 20, transcendentals=0
        ),
    )(words, gathered)


def sum_kernel(part, whole, keep, send):
    core = lax.axis_index("c")
    total = part[0]
    for index in range(1, part.shape[0]):
        total += part[index]
    whole[...] = total.astype(BF16)
    for block in range(2):
        for target, which in ((keep, core), (send, 1 - core)):
            start = pl.multiple_of(block * 128 + which * 64, 64)
            target[block * 64 : (block + 1) * 64, :] = whole[pl.ds(start, 64), :]


def sum_parts(part):
    _, rows, width = part.shape
    shapes = [(rows, width), (rows // 2, width), (rows // 2, width)]
    return pl.pallas_call(
        sum_kernel,
        out_shape=[jax.ShapeDtypeStruct(shape, BF16) for shape in shapes],
        compiler_params=pltpu.CompilerParams(vmem_limit_bytes=8 << 20),
    )(part)


RING = (0, -1, -2, -3, -4, 1, 2, 3)


def condition_kernel(*refs):
    low, high, (mine, other), (out, pieces, tiles, arrived) = refs[0], refs[1:9], refs[9:11], refs[11:]
    core = lax.axis_index("c")
    yl = lax.axis_index("yl")
    z = lax.axis_index("zh") * 2 + lax.axis_index("zl")
    zl = lax.axis_index("zl")
    tile_copies = []
    for group in range(2):
        rows = pl.ds(pl.multiple_of((zl ^ group) * 512, 512), 512)
        for which, (source, place) in enumerate(((mine, core), (other, 1 - core))):
            tile_copies.append(
                pltpu.make_async_copy(
                    source.at[rows, :], tiles.at[place, rows, :], arrived.at[16 + group * 2 + which]
                )
            )
    copies = []
    for index, away in enumerate(RING):
        for run, source in enumerate((low.at[(z + (away + 8)) & 7], high[index])):
            target = pieces.at[index, :, :, run * 128 : (run + 1) * 128]
            copies.append(pltpu.make_async_copy(source, target, arrived.at[index * 2 + run]))
    for group in range(2):
        for copy in tile_copies[group * 2 : group * 2 + 2]:
            copy.start()
        for index, away in enumerate(RING):
            if away % 2 == group:
                copies[index * 2].start()
                copies[index * 2 + 1].start()
    for group in range(2):
        for copy in tile_copies[group * 2 : group * 2 + 2]:
            copy.wait()
        for index, away in enumerate(RING):
            if away % 2 != group:
                continue
            copies[index * 2].wait()
            copies[index * 2 + 1].wait()
            source = (z + (away + 8)) & 7
            total = None
            for flip in range(4):
                start = pl.multiple_of(((zl ^ group) * 2 + (core ^ (flip % 2))) * 256, 256)
                tile = tiles[yl ^ (flip // 2), pl.ds(start, 256), :]
                term = jnp.dot(pieces[index, flip], tile, preferred_element_type=F32)
                total = term if total is None else total + term
            at = pl.ds(pl.multiple_of((source >> 1) * 128, 128), 128)
            if group == 0:
                out[at, :] = total
            else:
                out[at, :] += total


def condition(low, high, mine, other):
    _, flips, rows, width = low.shape
    return pl.pallas_call(
        condition_kernel,
        out_shape=jax.ShapeDtypeStruct((4 * rows, mine.shape[1]), F32),
        in_specs=[pl.BlockSpec(memory_space=pltpu.HBM)] * 11,
        out_specs=pl.BlockSpec(memory_space=pltpu.VMEM),
        scratch_shapes=[
            pltpu.VMEM((8, flips, rows, 2 * width), BF16),
            pltpu.VMEM((2,) + mine.shape, BF16),
            pltpu.SemaphoreType.DMA((20,)),
        ],
        compiler_params=pltpu.CompilerParams(vmem_limit_bytes=60 << 20),
        cost_estimate=pl.CostEstimate(flops=2 * 512 * 2048 * 1024, bytes_accessed=7 << 20, transcendentals=0),
    )(low, *high, mine, other)


def join_kernel(*refs):
    for index, ref in enumerate(refs[:-1]):
        refs[-1][index] = ref[...]


def join(values):
    return pl.pallas_call(
        join_kernel,
        out_shape=jax.ShapeDtypeStruct((len(values),) + values[0].shape, values[0].dtype),
        compiler_params=pltpu.CompilerParams(vmem_limit_bytes=6 << 20),
    )(*values)


def pair_kernel(parts, *refs):
    features, (out, rows, pairs) = refs[:2], refs[2:]
    yh, core = lax.axis_index("yh"), lax.axis_index("c")
    place = lax.axis_index("zh") * 2 + lax.axis_index("zl")
    total = parts[0]
    for index in range(1, parts.shape[0]):
        total += parts[index]
    rows[...] = total.astype(BF16)
    pairs[...] = jnp.zeros_like(pairs)
    for x in range(4):
        for flip_yh in range(2):
            source = (yh * 4 + x) ^ (flip_yh * 4) ^ place
            value = None
            for flip_core in range(2):
                start = pl.multiple_of(((source & 1) * 2 + (core ^ flip_core)) * 256, 256)
                held = features[flip_core].at[x]
                term = lax.dot_general(
                    rows[:, pl.ds(start, 256)],
                    jnp.concatenate([held[flip_yh * 2], held[flip_yh * 2 + 1]], axis=1),
                    (((1,), (1,)), ((), ())),
                    preferred_element_type=F32,
                )
                value = term if value is None else value + term
            pairs[:, pl.ds(pl.multiple_of((source >> 1) * 256, 256), 256)] += value
    for block in range(16):
        piece = pairs[:, block * 64 : (block + 1) * 64]
        out[block, :, :64] = piece[:32]
        out[block, :, 64:] = piece[32:]


def pair(parts, near, far):
    return pl.pallas_call(
        pair_kernel,
        out_shape=jax.ShapeDtypeStruct((16, 32, 128), F32),
        scratch_shapes=[pltpu.VMEM((64, 1024), BF16), pltpu.VMEM((64, 1024), F32)],
        compiler_params=pltpu.CompilerParams(vmem_limit_bytes=12 << 20),
    )(parts, near, far)


def finish_kernel(parts, out):
    total = parts[0]
    for index in range(1, parts.shape[0]):
        total += parts[index]
    total = total * SCALE
    out[:32] = total[:, :64]
    out[32:] = total[:, 64:]


def finish(parts):
    return pl.pallas_call(finish_kernel, out_shape=jax.ShapeDtypeStruct((64, 64), F32))(parts)


def swap(value, axis):
    return lax.ppermute(value, axis, [(0, 1), (1, 0)])


def step_z(value, by):
    return lax.ppermute(value, ("zh", "zl"), [(i, (i + by) % 8) for i in range(8)])


def ring(value, beside):
    up = [step_z(value, 1)]
    down = [step_z(value, 7)]
    up.append(step_z(up[0], 1))
    down.append(step_z(down[0], 7))
    beside, up[1], down[1] = lax.optimization_barrier((beside, up[1], down[1]))
    up.append(step_z(up[1], 1))
    down.append(step_z(down[1], 7))
    up.append(step_z(up[2], 1))
    return beside, [value] + up + down


def flips(keep, send):
    received = swap(send, "c")
    return join([keep, received, swap(keep, "yl"), swap(received, "yl")])


def per_device(gradients, inverse_gram, hash_words):
    half = gradients.shape[0] // 2
    width, depth, params = 128, 1024, 2 * gradients.shape[1]
    split = 5
    first = table(0, width, 0, split, depth, params, hash_words)
    second = table(0, width, split, params // depth - split, depth, params, hash_words)

    next_y = swap(gradients, "yl")
    next_z = swap(gradients, "zl")
    first, next_y, next_z = lax.optimization_barrier((first, next_y, next_z))
    diag_a, diag_b = swap(next_y[:half], "zl"), swap(next_z[half:], "yl")
    diag_a, diag_b, second = lax.optimization_barrier((diag_a, diag_b, second))
    own = [gradients, next_y, next_z, diag_a, diag_b]
    blocks = own + [swap(a, "c") for a in own]
    other_tile = swap(inverse_gram, "c")

    partial, gathered = project_ready(first, second, width, blocks)
    part = lax.all_to_all(partial, CHIPS, 0, 0, tiled=True)
    partial = project_hash(1, width, hash_words, gathered)
    partial, part = lax.optimization_barrier((partial, part))
    next_part = lax.all_to_all(partial, CHIPS, 0, 0, tiled=True)

    def turn(value):
        return [
            lax.ppermute(
                value,
                EX + PAR,
                [
                    (((z * 2 + yl) * 8 + chip) * 2 + c, ((chip * 2 + yl) * 8 + (z ^ chip ^ flip)) * 2 + c)
                    for z in range(8)
                    for yl in range(2)
                    for chip in range(8)
                    for c in range(2)
                ],
            )
            for flip in (0, 4)
        ]

    whole, keep, send = sum_parts(part)
    mine = flips(keep, send)
    low = lax.all_gather(mine, ("zh", "zl"), axis=0)
    turned = turn(whole)
    next_part, mine, turned = lax.optimization_barrier((next_part, mine, turned))
    whole, keep, send = sum_parts(next_part)
    whole, mine = lax.optimization_barrier((whole, flips(keep, send)))
    next_turned, high = ring(mine, turn(whole))
    near = join([turned[0], next_turned[0], turned[1], next_turned[1]])
    near, low = lax.optimization_barrier((near, low))
    near = lax.all_gather(near, "x", axis=0)
    conditioned = condition(low, high, inverse_gram, other_tile)
    parts = lax.all_to_all(conditioned.reshape(8, 64, 1024), CHIPS, 0, 0, tiled=True)
    return finish(lax.all_to_all(pair(parts, near, swap(near, "c")), EX, 0, 0, tiled=True))


def solution(mesh):
    fine = Mesh(mesh.devices.reshape(4, 2, 2, 2, 4, 2), EX + PAR)
    return jax.shard_map(
        per_device,
        mesh=fine,
        in_specs=(P(EX, PAR), P(PAR, EX), P()),
        out_specs=P(PAR, EX),
        check_vma=False,
    )
```

```python
import functools

import jax
import jax.numpy as jnp
from jax import lax
from jax.experimental import pallas as pl
from jax.experimental.pallas import tpu as pltpu
from jax.sharding import Mesh
from jax.sharding import PartitionSpec as P

FEATURES = 16384
SCALE = FEATURES ** (-0.5)
BF16 = jnp.bfloat16
F32 = jnp.float32

EX = ("zh", "zl", "yl")
CHIPS = ("yh", "x")
PAR = ("yh", "x", "c")
FEATURES_PER_CHIP = FEATURES // 8


def shifted(values, amount):
    return lax.shift_right_logical(values, jnp.full(values.shape, amount, jnp.int32))


def signs(hash_words, row_start, rows, cols):
    m0 = hash_words[0] | 1
    row_ids = lax.broadcasted_iota(jnp.int32, (rows, cols.shape[1]), 0)
    mixed = row_ids * (FEATURES * m0) + (cols * m0 + (row_start * (FEATURES * m0) + hash_words[1]))
    mixed = mixed ^ shifted(mixed, 15)
    mixed = mixed * (hash_words[2] | 1)
    mixed = mixed ^ shifted(mixed, 13)
    mixed = mixed * (hash_words[3] | 1)
    return jnp.where(mixed < 0, BF16(-1), BF16(1))


def columns(first, count, part, width):
    slice_id = lax.axis_index("yl") * 4 + lax.axis_index("zl") * 2 + lax.axis_index("c")
    column = lax.broadcasted_iota(jnp.int32, (1, count), 1)
    group, within = column // width, column % width
    return (group + first // width) * FEATURES_PER_CHIP + within + (slice_id * 256 + part * width)


def first_parameter(block, depth, params):
    per_core = params // 2 // depth
    core = lax.axis_index("c")
    chip = lax.axis_index("yh") * 4 + lax.axis_index("x")
    which = jnp.where(block < per_core, core, 1 - core)
    inner = jnp.where(block < per_core, block, block - per_core)
    return (chip * 2 + which) * (params // 2) + inner * depth


def table_kernel(part, width, first, params, words, out):
    depth, wide = out.shape
    row_start = first_parameter(pl.program_id(0) + first, depth, params)
    rows = 32

    def chunk(index, carry):
        start = pl.multiple_of(index * rows, rows)
        cols = columns(0, wide, part, width)
        out[pl.ds(start, rows), :] = signs(words, row_start + start, rows, cols)
        return carry

    lax.fori_loop(0, depth // rows, chunk, 0)


def table(part, width, first, count, depth, params, words):
    return pl.pallas_call(
        functools.partial(table_kernel, part, width, first, params),
        out_shape=jax.ShapeDtypeStruct((count * depth, 8 * width), BF16),
        grid=(count,),
        in_specs=[pl.BlockSpec(memory_space=pltpu.SMEM)],
        out_specs=pl.BlockSpec((depth, 8 * width), lambda k: (k, 0)),
        compiler_params=pltpu.CompilerParams(vmem_limit_bytes=12 << 20),
        cost_estimate=pl.CostEstimate(
            flops=1200 * count * depth * 8 * width,
            bytes_accessed=2 * count * depth * 8 * width,
            transcendentals=0,
        ),
    )(words)


def load_examples(blocks, examples, arrived):
    me = lax.axis_index("zl") * 2 + lax.axis_index("yl")
    half = len(blocks) // 2
    params = blocks[0].shape[1]
    rows = blocks[0].shape[0]
    copies = []
    for index, block in enumerate(blocks):
        kind = index % half
        start = (me ^ min(kind, 3)) * rows + (rows // 2 if kind == 4 else 0)
        target = examples.at[
            pl.ds(pl.multiple_of(start, 32), block.shape[0]),
            (index // half) * params : (index // half + 1) * params,
        ]
        copies.append(pltpu.make_async_copy(block, target, arrived.at[index]))
    for copy in copies:
        copy.start()
    for copy in copies:
        copy.wait()


def write_run(out, total, width):
    for block in range(8):
        out[block] = total[:, block * width : (block + 1) * width] * SCALE


def ready_kernel(split, width, first, second, *refs):
    blocks, (out, gathered, examples, total, arrived) = refs[:-5], refs[-5:]
    step = pl.program_id(0)
    depth = first.shape[0]
    hand_on = pltpu.make_async_copy(examples, gathered, arrived.at[len(blocks)])

    @pl.when(step == 0)
    def _():
        load_examples(blocks, examples, arrived)
        hand_on.start()
        total[...] = jnp.zeros_like(total)

    held = examples[:, pl.ds(pl.multiple_of(step * depth, depth), depth)]

    @pl.when(step < split)
    def _():
        total[...] += jnp.dot(held, first[...], preferred_element_type=F32)

    @pl.when(step >= split)
    def _():
        total[...] += jnp.dot(held, second[...], preferred_element_type=F32)

    @pl.when(step == pl.num_programs(0) - 1)
    def _():
        hand_on.wait()
        write_run(out, total, width)


def project_ready(first, second, width, blocks):
    rows, params = 4 * blocks[0].shape[0], 2 * blocks[0].shape[1]
    depth = 1024
    split = first.shape[0] // depth
    return pl.pallas_call(
        functools.partial(ready_kernel, split, width),
        out_shape=[
            jax.ShapeDtypeStruct((8, rows, width), F32),
            jax.ShapeDtypeStruct((rows, params), BF16),
        ],
        grid=(params // depth,),
        in_specs=[
            pl.BlockSpec((depth, 8 * width), lambda k: (jnp.minimum(k, split - 1), 0)),
            pl.BlockSpec((depth, 8 * width), lambda k: (jnp.maximum(k - split, 0), 0)),
        ]
        + [pl.BlockSpec(memory_space=pltpu.HBM)] * len(blocks),
        out_specs=[
            pl.BlockSpec((8, rows, width), lambda k: (0, 0, 0)),
            pl.BlockSpec(memory_space=pltpu.HBM),
        ],
        scratch_shapes=[
            pltpu.VMEM((rows, params), BF16),
            pltpu.VMEM((rows, 8 * width), F32),
            pltpu.SemaphoreType.DMA((len(blocks) + 1,)),
        ],
        compiler_params=pltpu.CompilerParams(vmem_limit_bytes=24 << 20),
        cost_estimate=pl.CostEstimate(
            flops=2 * rows * params * 8 * width, bytes_accessed=16 << 20, transcendentals=0
        ),
    )(first, second, *blocks)


def hash_kernel(part, width, words, gathered, out, examples, total, arrived):
    step = pl.program_id(0)
    steps = arrived.shape[0]
    params = examples.shape[1]
    depth = params // steps
    wide = 512

    def bring(index):
        at = pl.ds(pl.multiple_of(index * depth, depth), depth)
        return pltpu.make_async_copy(gathered.at[:, at], examples.at[:, at], arrived.at[index])

    @pl.when(step == 0)
    def _():
        for index in range(steps):
            bring(index).start()
        total[...] = jnp.zeros_like(total)

    bring(step).wait()
    held = examples[:, pl.ds(pl.multiple_of(step * depth, depth), depth)]
    row_start = first_parameter(step, depth, params)
    for first in range(0, 8 * width, wide):
        made = signs(words, row_start, depth, columns(first, wide, part, width))
        total[:, first : first + wide] += jnp.dot(held, made, preferred_element_type=F32)

    @pl.when(step == steps - 1)
    def _():
        write_run(out, total, width)


def project_hash(part, width, words, gathered, steps=16):
    rows, params = gathered.shape
    return pl.pallas_call(
        functools.partial(hash_kernel, part, width),
        out_shape=jax.ShapeDtypeStruct((8, rows, width), F32),
        grid=(steps,),
        in_specs=[pl.BlockSpec(memory_space=pltpu.SMEM), pl.BlockSpec(memory_space=pltpu.HBM)],
        out_specs=pl.BlockSpec((8, rows, width), lambda k: (0, 0, 0)),
        scratch_shapes=[
            pltpu.VMEM((rows, params), BF16),
            pltpu.VMEM((rows, 8 * width), F32),
            pltpu.SemaphoreType.DMA((steps,)),
        ],
        compiler_params=pltpu.CompilerParams(vmem_limit_bytes=60 << 20),
        cost_estimate=pl.CostEstimate(
            flops=2 * rows * params * 8 * width, bytes_accessed=16 << 20, transcendentals=0
        ),
    )(words, gathered)


def sum_kernel(part, whole, keep, send):
    core = lax.axis_index("c")
    total = part[0]
    for index in range(1, part.shape[0]):
        total += part[index]
    whole[...] = total.astype(BF16)
    for block in range(2):
        for target, which in ((keep, core), (send, 1 - core)):
            start = pl.multiple_of(block * 128 + which * 64, 64)
            target[block * 64 : (block + 1) * 64, :] = whole[pl.ds(start, 64), :]


def sum_parts(part):
    _, rows, width = part.shape
    shapes = [(rows, width), (rows // 2, width), (rows // 2, width)]
    return pl.pallas_call(
        sum_kernel,
        out_shape=[jax.ShapeDtypeStruct(shape, BF16) for shape in shapes],
        compiler_params=pltpu.CompilerParams(vmem_limit_bytes=8 << 20),
    )(part)


RING = (0, -1, -2, -3, -4, 1, 2, 3)


def condition_kernel(*refs):
    low, high, (mine, other), (out, pieces, tiles, arrived) = refs[0], refs[1:9], refs[9:11], refs[11:]
    core = lax.axis_index("c")
    yl = lax.axis_index("yl")
    z = lax.axis_index("zh") * 2 + lax.axis_index("zl")
    zl = lax.axis_index("zl")
    tile_copies = []
    for group in range(2):
        rows = pl.ds(pl.multiple_of((zl ^ group) * 512, 512), 512)
        for which, (source, place) in enumerate(((mine, core), (other, 1 - core))):
            tile_copies.append(
                pltpu.make_async_copy(
                    source.at[rows, :], tiles.at[place, rows, :], arrived.at[16 + group * 2 + which]
                )
            )
    copies = []
    for index, away in enumerate(RING):
        for run, source in enumerate((low.at[(z + (away + 8)) & 7], high[index])):
            target = pieces.at[index, :, :, run * 128 : (run + 1) * 128]
            copies.append(pltpu.make_async_copy(source, target, arrived.at[index * 2 + run]))
    for group in range(2):
        for copy in tile_copies[group * 2 : group * 2 + 2]:
            copy.start()
        for index, away in enumerate(RING):
            if away % 2 == group:
                copies[index * 2].start()
                copies[index * 2 + 1].start()
    for group in range(2):
        for copy in tile_copies[group * 2 : group * 2 + 2]:
            copy.wait()
        for index, away in enumerate(RING):
            if away % 2 != group:
                continue
            copies[index * 2].wait()
            copies[index * 2 + 1].wait()
            source = (z + (away + 8)) & 7
            total = None
            for flip in range(4):
                start = pl.multiple_of(((zl ^ group) * 2 + (core ^ (flip % 2))) * 256, 256)
                tile = tiles[yl ^ (flip // 2), pl.ds(start, 256), :]
                term = jnp.dot(pieces[index, flip], tile, preferred_element_type=F32)
                total = term if total is None else total + term
            at = pl.ds(pl.multiple_of((source >> 1) * 128, 128), 128)
            if group == 0:
                out[at, :] = total
            else:
                out[at, :] += total


def condition(low, high, mine, other):
    _, flips, rows, width = low.shape
    return pl.pallas_call(
        condition_kernel,
        out_shape=jax.ShapeDtypeStruct((4 * rows, mine.shape[1]), F32),
        in_specs=[pl.BlockSpec(memory_space=pltpu.HBM)] * 11,
        out_specs=pl.BlockSpec(memory_space=pltpu.VMEM),
        scratch_shapes=[
            pltpu.VMEM((8, flips, rows, 2 * width), BF16),
            pltpu.VMEM((2,) + mine.shape, BF16),
            pltpu.SemaphoreType.DMA((20,)),
        ],
        compiler_params=pltpu.CompilerParams(vmem_limit_bytes=60 << 20),
        cost_estimate=pl.CostEstimate(flops=2 * 512 * 2048 * 1024, bytes_accessed=7 << 20, transcendentals=0),
    )(low, *high, mine, other)


def join_kernel(*refs):
    for index, ref in enumerate(refs[:-1]):
        refs[-1][index] = ref[...]


def join(values):
    return pl.pallas_call(
        join_kernel,
        out_shape=jax.ShapeDtypeStruct((len(values),) + values[0].shape, values[0].dtype),
        compiler_params=pltpu.CompilerParams(vmem_limit_bytes=6 << 20),
    )(*values)


def pair_kernel(parts, *refs):
    features, (out, rows, pairs) = refs[:2], refs[2:]
    yh, core = lax.axis_index("yh"), lax.axis_index("c")
    place = lax.axis_index("zh") * 2 + lax.axis_index("zl")
    total = parts[0]
    for index in range(1, parts.shape[0]):
        total += parts[index]
    rows[...] = total.astype(BF16)
    pairs[...] = jnp.zeros_like(pairs)
    for x in range(4):
        for flip_yh in range(2):
            source = (yh * 4 + x) ^ (flip_yh * 4) ^ place
            value = None
            for flip_core in range(2):
                start = pl.multiple_of(((source & 1) * 2 + (core ^ flip_core)) * 256, 256)
                held = features[flip_core].at[x]
                term = lax.dot_general(
                    rows[:, pl.ds(start, 256)],
                    jnp.concatenate([held[flip_yh, 0], held[flip_yh, 1]], axis=1),
                    (((1,), (1,)), ((), ())),
                    preferred_element_type=F32,
                )
                value = term if value is None else value + term
            pairs[:, pl.ds(pl.multiple_of((source >> 1) * 256, 256), 256)] += value
    for block in range(16):
        piece = pairs[:, block * 64 : (block + 1) * 64]
        out[block, :, :64] = piece[:32]
        out[block, :, 64:] = piece[32:]


def pair(parts, near, far):
    return pl.pallas_call(
        pair_kernel,
        out_shape=jax.ShapeDtypeStruct((16, 32, 128), F32),
        scratch_shapes=[pltpu.VMEM((64, 1024), BF16), pltpu.VMEM((64, 1024), F32)],
        compiler_params=pltpu.CompilerParams(vmem_limit_bytes=12 << 20),
    )(parts, near, far)


def finish_kernel(parts, out):
    total = parts[0]
    for index in range(1, parts.shape[0]):
        total += parts[index]
    total = total * SCALE
    out[:32] = total[:, :64]
    out[32:] = total[:, 64:]


def finish(parts):
    return pl.pallas_call(finish_kernel, out_shape=jax.ShapeDtypeStruct((64, 64), F32))(parts)


def swap(value, axis):
    return lax.ppermute(value, axis, [(0, 1), (1, 0)])


def step_z(value, by):
    return lax.ppermute(value, ("zh", "zl"), [(i, (i + by) % 8) for i in range(8)])


def ring(value):
    up = [step_z(value, 1)]
    down = [step_z(value, 7)]
    for _ in range(2):
        up.append(step_z(up[-1], 1))
        down.append(step_z(down[-1], 7))
    up.append(step_z(up[-1], 1))
    return [value] + up + down


def flips(keep, send):
    received = swap(send, "c")
    return join([keep, received, swap(keep, "yl"), swap(received, "yl")])


def per_device(gradients, inverse_gram, hash_words):
    half = gradients.shape[0] // 2
    width, depth, params = 128, 1024, 2 * gradients.shape[1]
    split = 5
    first = table(0, width, 0, split, depth, params, hash_words)
    second = table(0, width, split, params // depth - split, depth, params, hash_words)

    next_y = swap(gradients, "yl")
    next_z = swap(gradients, "zl")
    first, next_y, next_z = lax.optimization_barrier((first, next_y, next_z))
    diag_a, diag_b = swap(next_y[:half], "zl"), swap(next_z[half:], "yl")
    diag_a, diag_b, second = lax.optimization_barrier((diag_a, diag_b, second))
    own = [gradients, next_y, next_z, diag_a, diag_b]
    blocks = own + [swap(a, "c") for a in own]
    other_tile = swap(inverse_gram, "c")

    partial, gathered = project_ready(first, second, width, blocks)
    part = lax.all_to_all(partial, CHIPS, 0, 0, tiled=True)
    partial = project_hash(1, width, hash_words, gathered)
    partial, part = lax.optimization_barrier((partial, part))
    next_part = lax.all_to_all(partial, CHIPS, 0, 0, tiled=True)

    def turn(value):
        return [
            lax.ppermute(
                value,
                EX + PAR,
                [
                    (((z * 2 + yl) * 8 + chip) * 2 + c, ((chip * 2 + yl) * 8 + (z ^ chip ^ flip)) * 2 + c)
                    for z in range(8)
                    for yl in range(2)
                    for chip in range(8)
                    for c in range(2)
                ],
            )
            for flip in (0, 4)
        ]

    whole, keep, send = sum_parts(part)
    mine = flips(keep, send)
    low = lax.all_gather(mine, ("zh", "zl"), axis=0)
    next_part, mine = lax.optimization_barrier((next_part, mine))
    next_whole, keep, send = sum_parts(next_part)
    next_whole, high = lax.optimization_barrier((next_whole, ring(flips(keep, send))))
    turned = turn(join([whole, next_whole]))
    conditioned = condition(low, high, inverse_gram, other_tile)
    conditioned, turned = lax.optimization_barrier((conditioned, turned))
    near = lax.all_gather(join(turned), "x", axis=0)
    parts = lax.all_to_all(conditioned.reshape(8, 64, 1024), CHIPS, 0, 0, tiled=True)
    return finish(lax.all_to_all(pair(parts, near, swap(near, "c")), EX, 0, 0, tiled=True))


def solution(mesh):
    fine = Mesh(mesh.devices.reshape(4, 2, 2, 2, 4, 2), EX + PAR)
    return jax.shard_map(
        per_device,
        mesh=fine,
        in_specs=(P(EX, PAR), P(PAR, EX), P()),
        out_specs=P(PAR, EX),
        check_vma=False,
    )
```

```python
import functools

import jax
import jax.numpy as jnp
from jax import lax
from jax.experimental import pallas as pl
from jax.experimental.pallas import tpu as pltpu
from jax.sharding import Mesh
from jax.sharding import PartitionSpec as P

FEATURES = 16384
SCALE = FEATURES ** (-0.5)
BF16 = jnp.bfloat16
F32 = jnp.float32

EX = ("zh", "zl", "yl")
CHIPS = ("yh", "x")
PAR = ("yh", "x", "c")
FEATURES_PER_CHIP = FEATURES // 8


def shifted(values, amount):
    return lax.shift_right_logical(values, jnp.full(values.shape, amount, jnp.int32))


def signs(hash_words, row_start, rows, cols):
    m0 = hash_words[0] | 1
    row_ids = lax.broadcasted_iota(jnp.int32, (rows, cols.shape[1]), 0)
    mixed = row_ids * (FEATURES * m0) + (cols * m0 + (row_start * (FEATURES * m0) + hash_words[1]))
    mixed = mixed ^ shifted(mixed, 15)
    mixed = mixed * (hash_words[2] | 1)
    mixed = mixed ^ shifted(mixed, 13)
    mixed = mixed * (hash_words[3] | 1)
    return jnp.where(mixed < 0, BF16(-1), BF16(1))


def columns(first, count, part, width):
    slice_id = lax.axis_index("yl") * 4 + lax.axis_index("zl") * 2 + lax.axis_index("c")
    column = lax.broadcasted_iota(jnp.int32, (1, count), 1)
    group, within = column // width, column % width
    return (group + first // width) * FEATURES_PER_CHIP + within + (slice_id * 256 + part * width)


def first_parameter(block, depth, params):
    per_core = params // 2 // depth
    core = lax.axis_index("c")
    chip = lax.axis_index("yh") * 4 + lax.axis_index("x")
    which = jnp.where(block < per_core, core, 1 - core)
    inner = jnp.where(block < per_core, block, block - per_core)
    return (chip * 2 + which) * (params // 2) + inner * depth


def table_kernel(part, width, first, params, words, out):
    depth, wide = out.shape
    row_start = first_parameter(pl.program_id(0) + first, depth, params)
    rows = 32

    def chunk(index, carry):
        start = pl.multiple_of(index * rows, rows)
        cols = columns(0, wide, part, width)
        out[pl.ds(start, rows), :] = signs(words, row_start + start, rows, cols)
        return carry

    lax.fori_loop(0, depth // rows, chunk, 0)


def table(part, width, first, count, depth, params, words):
    return pl.pallas_call(
        functools.partial(table_kernel, part, width, first, params),
        out_shape=jax.ShapeDtypeStruct((count * depth, 8 * width), BF16),
        grid=(count,),
        in_specs=[pl.BlockSpec(memory_space=pltpu.SMEM)],
        out_specs=pl.BlockSpec((depth, 8 * width), lambda k: (k, 0)),
        compiler_params=pltpu.CompilerParams(vmem_limit_bytes=12 << 20),
        cost_estimate=pl.CostEstimate(
            flops=1200 * count * depth * 8 * width,
            bytes_accessed=2 * count * depth * 8 * width,
            transcendentals=0,
        ),
    )(words)


def load_examples(blocks, examples, arrived):
    me = lax.axis_index("zl") * 2 + lax.axis_index("yl")
    half = len(blocks) // 2
    params = blocks[0].shape[1]
    rows = blocks[0].shape[0]
    copies = []
    for index, block in enumerate(blocks):
        kind = index % half
        start = (me ^ min(kind, 3)) * rows + (rows // 2 if kind == 4 else 0)
        target = examples.at[
            pl.ds(pl.multiple_of(start, 32), block.shape[0]),
            (index // half) * params : (index // half + 1) * params,
        ]
        copies.append(pltpu.make_async_copy(block, target, arrived.at[index]))
    for copy in copies:
        copy.start()
    for copy in copies:
        copy.wait()


def write_run(out, total, width):
    for block in range(8):
        out[block] = total[:, block * width : (block + 1) * width] * SCALE


def ready_kernel(split, width, first, second, *refs):
    blocks, (out, gathered, examples, total, arrived) = refs[:-5], refs[-5:]
    step = pl.program_id(0)
    depth = first.shape[0]
    hand_on = pltpu.make_async_copy(examples, gathered, arrived.at[len(blocks)])

    @pl.when(step == 0)
    def _():
        load_examples(blocks, examples, arrived)
        hand_on.start()
        total[...] = jnp.zeros_like(total)

    held = examples[:, pl.ds(pl.multiple_of(step * depth, depth), depth)]

    @pl.when(step < split)
    def _():
        total[...] += jnp.dot(held, first[...], preferred_element_type=F32)

    @pl.when(step >= split)
    def _():
        total[...] += jnp.dot(held, second[...], preferred_element_type=F32)

    @pl.when(step == pl.num_programs(0) - 1)
    def _():
        hand_on.wait()
        write_run(out, total, width)


def project_ready(first, second, width, blocks):
    rows, params = 4 * blocks[0].shape[0], 2 * blocks[0].shape[1]
    depth = 1024
    split = first.shape[0] // depth
    return pl.pallas_call(
        functools.partial(ready_kernel, split, width),
        out_shape=[
            jax.ShapeDtypeStruct((8, rows, width), F32),
            jax.ShapeDtypeStruct((rows, params), BF16),
        ],
        grid=(params // depth,),
        in_specs=[
            pl.BlockSpec((depth, 8 * width), lambda k: (jnp.minimum(k, split - 1), 0)),
            pl.BlockSpec((depth, 8 * width), lambda k: (jnp.maximum(k - split, 0), 0)),
        ]
        + [pl.BlockSpec(memory_space=pltpu.HBM)] * len(blocks),
        out_specs=[
            pl.BlockSpec((8, rows, width), lambda k: (0, 0, 0)),
            pl.BlockSpec(memory_space=pltpu.HBM),
        ],
        scratch_shapes=[
            pltpu.VMEM((rows, params), BF16),
            pltpu.VMEM((rows, 8 * width), F32),
            pltpu.SemaphoreType.DMA((len(blocks) + 1,)),
        ],
        compiler_params=pltpu.CompilerParams(vmem_limit_bytes=24 << 20),
        cost_estimate=pl.CostEstimate(
            flops=2 * rows * params * 8 * width, bytes_accessed=16 << 20, transcendentals=0
        ),
    )(first, second, *blocks)


def hash_kernel(part, width, words, gathered, out, examples, total, arrived):
    step = pl.program_id(0)
    steps = arrived.shape[0]
    params = examples.shape[1]
    depth = params // steps
    wide = 512

    def bring(index):
        at = pl.ds(pl.multiple_of(index * depth, depth), depth)
        return pltpu.make_async_copy(gathered.at[:, at], examples.at[:, at], arrived.at[index])

    @pl.when(step == 0)
    def _():
        for index in range(steps):
            bring(index).start()
        total[...] = jnp.zeros_like(total)

    bring(step).wait()
    held = examples[:, pl.ds(pl.multiple_of(step * depth, depth), depth)]
    row_start = first_parameter(step, depth, params)
    for first in range(0, 8 * width, wide):
        made = signs(words, row_start, depth, columns(first, wide, part, width))
        total[:, first : first + wide] += jnp.dot(held, made, preferred_element_type=F32)

    @pl.when(step == steps - 1)
    def _():
        write_run(out, total, width)


def project_hash(part, width, words, gathered, steps=16):
    rows, params = gathered.shape
    return pl.pallas_call(
        functools.partial(hash_kernel, part, width),
        out_shape=jax.ShapeDtypeStruct((8, rows, width), F32),
        grid=(steps,),
        in_specs=[pl.BlockSpec(memory_space=pltpu.SMEM), pl.BlockSpec(memory_space=pltpu.HBM)],
        out_specs=pl.BlockSpec((8, rows, width), lambda k: (0, 0, 0)),
        scratch_shapes=[
            pltpu.VMEM((rows, params), BF16),
            pltpu.VMEM((rows, 8 * width), F32),
            pltpu.SemaphoreType.DMA((steps,)),
        ],
        compiler_params=pltpu.CompilerParams(vmem_limit_bytes=60 << 20),
        cost_estimate=pl.CostEstimate(
            flops=2 * rows * params * 8 * width, bytes_accessed=16 << 20, transcendentals=0
        ),
    )(words, gathered)


def sum_kernel(part, keep, send, whole):
    core = lax.axis_index("c")
    total = part[0]
    for index in range(1, part.shape[0]):
        total += part[index]
    whole[...] = total.astype(BF16)
    for block in range(2):
        for target, which in ((keep, core), (send, 1 - core)):
            start = pl.multiple_of(block * 128 + which * 64, 64)
            target[block * 64 : (block + 1) * 64, :] = whole[pl.ds(start, 64), :]


def sum_parts(part):
    _, rows, width = part.shape
    shapes = [(rows // 2, width), (rows // 2, width)]
    return pl.pallas_call(
        sum_kernel,
        out_shape=[jax.ShapeDtypeStruct(shape, BF16) for shape in shapes],
        scratch_shapes=[pltpu.VMEM((rows, width), BF16)],
        compiler_params=pltpu.CompilerParams(vmem_limit_bytes=8 << 20),
    )(part)


RING = (0, -1, -2, -3, -4, 1, 2, 3)


def condition_kernel(*refs):
    low, high, (mine, other), (out, pieces, tiles, arrived) = refs[0], refs[1:9], refs[9:11], refs[11:]
    core = lax.axis_index("c")
    yl = lax.axis_index("yl")
    z = lax.axis_index("zh") * 2 + lax.axis_index("zl")
    zl = lax.axis_index("zl")
    tile_copies = []
    for group in range(2):
        rows = pl.ds(pl.multiple_of((zl ^ group) * 512, 512), 512)
        for which, (source, place) in enumerate(((mine, core), (other, 1 - core))):
            tile_copies.append(
                pltpu.make_async_copy(
                    source.at[rows, :], tiles.at[place, rows, :], arrived.at[16 + group * 2 + which]
                )
            )
    copies = []
    for index, away in enumerate(RING):
        for run, source in enumerate((low.at[(z + (away + 8)) & 7], high[index])):
            target = pieces.at[index, :, :, run * 128 : (run + 1) * 128]
            copies.append(pltpu.make_async_copy(source, target, arrived.at[index * 2 + run]))
    for group in range(2):
        for copy in tile_copies[group * 2 : group * 2 + 2]:
            copy.start()
        for index, away in enumerate(RING):
            if away % 2 == group:
                copies[index * 2].start()
                copies[index * 2 + 1].start()
    for group in range(2):
        for copy in tile_copies[group * 2 : group * 2 + 2]:
            copy.wait()
        for index, away in enumerate(RING):
            if away % 2 != group:
                continue
            copies[index * 2].wait()
            copies[index * 2 + 1].wait()
            source = (z + (away + 8)) & 7
            total = None
            for flip in range(4):
                start = pl.multiple_of(((zl ^ group) * 2 + (core ^ (flip % 2))) * 256, 256)
                tile = tiles[yl ^ (flip // 2), pl.ds(start, 256), :]
                term = jnp.dot(pieces[index, flip], tile, preferred_element_type=F32)
                total = term if total is None else total + term
            at = pl.ds(pl.multiple_of((source >> 1) * 128, 128), 128)
            if group == 0:
                out[at, :] = total
            else:
                out[at, :] += total


def condition(low, high, mine, other):
    _, flips, rows, width = low.shape
    return pl.pallas_call(
        condition_kernel,
        out_shape=jax.ShapeDtypeStruct((4 * rows, mine.shape[1]), F32),
        in_specs=[pl.BlockSpec(memory_space=pltpu.HBM)] * 11,
        out_specs=pl.BlockSpec(memory_space=pltpu.VMEM),
        scratch_shapes=[
            pltpu.VMEM((8, flips, rows, 2 * width), BF16),
            pltpu.VMEM((2,) + mine.shape, BF16),
            pltpu.SemaphoreType.DMA((20,)),
        ],
        compiler_params=pltpu.CompilerParams(vmem_limit_bytes=60 << 20),
        cost_estimate=pl.CostEstimate(flops=2 * 512 * 2048 * 1024, bytes_accessed=7 << 20, transcendentals=0),
    )(low, *high, mine, other)


def join_kernel(*refs):
    for index, ref in enumerate(refs[:-1]):
        refs[-1][index] = ref[...]


def join(values):
    return pl.pallas_call(
        join_kernel,
        out_shape=jax.ShapeDtypeStruct((len(values),) + values[0].shape, values[0].dtype),
        compiler_params=pltpu.CompilerParams(vmem_limit_bytes=6 << 20),
    )(*values)


def pack_kernel(low, *refs):
    high, (out, arrived) = refs[:8], refs[8:]
    z = lax.axis_index("zh") * 2 + lax.axis_index("zl")
    copies = []
    for index, away in enumerate(RING):
        for run, source in enumerate((low.at[(z + (away + 8)) & 7, 0:2], high[index].at[0:2])):
            copies.append(pltpu.make_async_copy(source, out.at[run, index], arrived.at[index * 2 + run]))
    for copy in copies:
        copy.start()
    for copy in copies:
        copy.wait()


def pack(low, high):
    _, _, rows, width = low.shape
    return pl.pallas_call(
        pack_kernel,
        out_shape=jax.ShapeDtypeStruct((2, 8, 2, rows, width), BF16),
        in_specs=[pl.BlockSpec(memory_space=pltpu.HBM)] * 9,
        out_specs=pl.BlockSpec(memory_space=pltpu.HBM),
        scratch_shapes=[pltpu.SemaphoreType.DMA((16,))],
        compiler_params=pltpu.CompilerParams(vmem_limit_bytes=4 << 20),
    )(low, *high)


def pair_kernel(parts, near, far, out, rows, pairs):
    core = lax.axis_index("c")
    place = lax.axis_index("zh") * 2 + lax.axis_index("zl")
    origin = (lax.axis_index("yh") * 4 + lax.axis_index("x")) ^ place
    total = parts[0]
    for index in range(1, parts.shape[0]):
        total += parts[index]
    rows[...] = total.astype(BF16)
    for half, held in enumerate((near, far)):
        for index, away in enumerate(RING):
            source = (origin + (away + 8)) & 7
            value = None
            for flip in range(2):
                start = ((source & 1) * 2 + (core ^ half ^ flip)) * 256
                term = lax.dot_general(
                    rows[:, pl.ds(pl.multiple_of(start, 256), 256)],
                    jnp.concatenate([held[0, index, flip], held[1, index, flip]], axis=1),
                    (((1,), (1,)), ((), ())),
                    preferred_element_type=F32,
                )
                value = term if value is None else value + term
            pairs[half, source] = value
    for half in range(2):
        for zh in range(4):
            value = pairs[half, zh * 2] + pairs[half, zh * 2 + 1]
            for block in range(2):
                piece = value[:, block * 64 : (block + 1) * 64]
                target = zh * 4 + block * 2 + (core ^ half)
                out[target, :, :64] = piece[:32]
                out[target, :, 64:] = piece[32:]


def pair(parts, near, far):
    return pl.pallas_call(
        pair_kernel,
        out_shape=jax.ShapeDtypeStruct((16, 32, 128), F32),
        scratch_shapes=[pltpu.VMEM((64, 1024), BF16), pltpu.VMEM((2, 8, 64, 128), F32)],
        compiler_params=pltpu.CompilerParams(vmem_limit_bytes=12 << 20),
    )(parts, near, far)


def finish_kernel(parts, out):
    total = parts[0]
    for index in range(1, parts.shape[0]):
        total += parts[index]
    total = total * SCALE
    out[:32] = total[:, :64]
    out[32:] = total[:, 64:]


def finish(parts):
    return pl.pallas_call(finish_kernel, out_shape=jax.ShapeDtypeStruct((64, 64), F32))(parts)


def swap(value, axis):
    return lax.ppermute(value, axis, [(0, 1), (1, 0)])


def step_z(value, by):
    return lax.ppermute(value, ("zh", "zl"), [(i, (i + by) % 8) for i in range(8)])


def ring(value):
    up = [step_z(value, 1)]
    down = [step_z(value, 7)]
    for _ in range(2):
        up.append(step_z(up[-1], 1))
        down.append(step_z(down[-1], 7))
    up.append(step_z(up[-1], 1))
    return [value] + up + down


def flips(keep, send):
    received = swap(send, "c")
    return join([keep, received, swap(keep, "yl"), swap(received, "yl")])


def per_device(gradients, inverse_gram, hash_words):
    half = gradients.shape[0] // 2
    width, depth, params = 128, 1024, 2 * gradients.shape[1]
    split = 5
    first = table(0, width, 0, split, depth, params, hash_words)
    second = table(0, width, split, params // depth - split, depth, params, hash_words)

    next_y = swap(gradients, "yl")
    next_z = swap(gradients, "zl")
    first, next_y, next_z = lax.optimization_barrier((first, next_y, next_z))
    diag_a, diag_b = swap(next_y[:half], "zl"), swap(next_z[half:], "yl")
    diag_a, diag_b, second = lax.optimization_barrier((diag_a, diag_b, second))
    own = [gradients, next_y, next_z, diag_a, diag_b]
    blocks = own + [swap(a, "c") for a in own]
    other_tile = swap(inverse_gram, "c")

    partial, gathered = project_ready(first, second, width, blocks)
    part = lax.all_to_all(partial, CHIPS, 0, 0, tiled=True)
    partial = project_hash(1, width, hash_words, gathered)
    partial, part = lax.optimization_barrier((partial, part))
    next_part = lax.all_to_all(partial, CHIPS, 0, 0, tiled=True)

    keep, send = sum_parts(part)
    mine = flips(keep, send)
    low = lax.all_gather(mine, ("zh", "zl"), axis=0)
    next_part, mine = lax.optimization_barrier((next_part, mine))
    high = ring(flips(*sum_parts(next_part)))

    route = [
        (((z * 2 + yl) * 8 + chip) * 2 + c, ((chip * 2 + yl) * 8 + (z ^ chip)) * 2 + c)
        for z in range(8)
        for yl in range(2)
        for chip in range(8)
        for c in range(2)
    ]
    packed = pack(low, high)
    packed, high = lax.optimization_barrier((packed, high))
    near = lax.ppermute(packed, EX + PAR, route)
    conditioned = condition(low, high, inverse_gram, other_tile)
    parts = lax.all_to_all(conditioned.reshape(8, 64, 1024), CHIPS, 0, 0, tiled=True)
    return finish(lax.all_to_all(pair(parts, near, swap(near, "c")), EX, 0, 0, tiled=True))


def solution(mesh):
    fine = Mesh(mesh.devices.reshape(4, 2, 2, 2, 4, 2), EX + PAR)
    return jax.shard_map(
        per_device,
        mesh=fine,
        in_specs=(P(EX, PAR), P(PAR, EX), P()),
        out_specs=P(PAR, EX),
        check_vma=False,
    )
```

```python
import functools

import jax
import jax.numpy as jnp
from jax import lax
from jax.experimental import pallas as pl
from jax.experimental.pallas import tpu as pltpu
from jax.sharding import Mesh
from jax.sharding import PartitionSpec as P

FEATURES = 16384
SCALE = FEATURES ** (-0.5)
BF16 = jnp.bfloat16
F32 = jnp.float32

EX = ("zh", "zl", "yl")
CHIPS = ("yh", "x")
PAR = ("yh", "x", "c")
FEATURES_PER_CHIP = FEATURES // 8


def shifted(values, amount):
    return lax.shift_right_logical(values, jnp.full(values.shape, amount, jnp.int32))


def signs(hash_words, row_start, rows, cols):
    m0 = hash_words[0] | 1
    row_ids = lax.broadcasted_iota(jnp.int32, (rows, cols.shape[1]), 0)
    mixed = row_ids * (FEATURES * m0) + (cols * m0 + (row_start * (FEATURES * m0) + hash_words[1]))
    mixed = mixed ^ shifted(mixed, 15)
    mixed = mixed * (hash_words[2] | 1)
    mixed = mixed ^ shifted(mixed, 13)
    mixed = mixed * (hash_words[3] | 1)
    return jnp.where(mixed < 0, BF16(-1), BF16(1))


def columns(first, count, part, width):
    slice_id = lax.axis_index("yl") * 4 + lax.axis_index("zl") * 2 + lax.axis_index("c")
    column = lax.broadcasted_iota(jnp.int32, (1, count), 1)
    group, within = column // width, column % width
    return (group + first // width) * FEATURES_PER_CHIP + within + (slice_id * 256 + part * width)


def first_parameter(block, depth, params):
    per_core = params // 2 // depth
    core = lax.axis_index("c")
    chip = lax.axis_index("yh") * 4 + lax.axis_index("x")
    which = jnp.where(block < per_core, core, 1 - core)
    inner = jnp.where(block < per_core, block, block - per_core)
    return (chip * 2 + which) * (params // 2) + inner * depth


def table_kernel(part, width, first, params, words, out):
    depth, wide = out.shape
    row_start = first_parameter(pl.program_id(0) + first, depth, params)
    rows = 32

    def chunk(index, carry):
        start = pl.multiple_of(index * rows, rows)
        cols = columns(0, wide, part, width)
        out[pl.ds(start, rows), :] = signs(words, row_start + start, rows, cols)
        return carry

    lax.fori_loop(0, depth // rows, chunk, 0)


def table(part, width, first, count, depth, params, words):
    return pl.pallas_call(
        functools.partial(table_kernel, part, width, first, params),
        out_shape=jax.ShapeDtypeStruct((count * depth, 8 * width), BF16),
        grid=(count,),
        in_specs=[pl.BlockSpec(memory_space=pltpu.SMEM)],
        out_specs=pl.BlockSpec((depth, 8 * width), lambda k: (k, 0)),
        compiler_params=pltpu.CompilerParams(vmem_limit_bytes=12 << 20),
        cost_estimate=pl.CostEstimate(
            flops=1200 * count * depth * 8 * width,
            bytes_accessed=2 * count * depth * 8 * width,
            transcendentals=0,
        ),
    )(words)


def load_examples(blocks, examples, arrived):
    me = lax.axis_index("zl") * 2 + lax.axis_index("yl")
    half = len(blocks) // 2
    params = blocks[0].shape[1]
    rows = blocks[0].shape[0]
    copies = []
    for index, block in enumerate(blocks):
        kind = index % half
        start = (me ^ min(kind, 3)) * rows + (rows // 2 if kind == 4 else 0)
        target = examples.at[
            pl.ds(pl.multiple_of(start, 32), block.shape[0]),
            (index // half) * params : (index // half + 1) * params,
        ]
        copies.append(pltpu.make_async_copy(block, target, arrived.at[index]))
    for copy in copies:
        copy.start()
    for copy in copies:
        copy.wait()


def write_run(out, total, width):
    for block in range(8):
        out[block] = total[:, block * width : (block + 1) * width] * SCALE


def ready_kernel(split, width, first, second, *refs):
    blocks, (out, gathered, examples, total, arrived) = refs[:-5], refs[-5:]
    step = pl.program_id(0)
    depth = first.shape[0]
    hand_on = pltpu.make_async_copy(examples, gathered, arrived.at[len(blocks)])

    @pl.when(step == 0)
    def _():
        load_examples(blocks, examples, arrived)
        hand_on.start()
        total[...] = jnp.zeros_like(total)

    held = examples[:, pl.ds(pl.multiple_of(step * depth, depth), depth)]

    @pl.when(step < split)
    def _():
        total[...] += jnp.dot(held, first[...], preferred_element_type=F32)

    @pl.when(step >= split)
    def _():
        total[...] += jnp.dot(held, second[...], preferred_element_type=F32)

    @pl.when(step == pl.num_programs(0) - 1)
    def _():
        hand_on.wait()
        write_run(out, total, width)


def project_ready(first, second, width, blocks):
    rows, params = 4 * blocks[0].shape[0], 2 * blocks[0].shape[1]
    depth = 1024
    split = first.shape[0] // depth
    return pl.pallas_call(
        functools.partial(ready_kernel, split, width),
        out_shape=[
            jax.ShapeDtypeStruct((8, rows, width), F32),
            jax.ShapeDtypeStruct((rows, params), BF16),
        ],
        grid=(params // depth,),
        in_specs=[
            pl.BlockSpec((depth, 8 * width), lambda k: (jnp.minimum(k, split - 1), 0)),
            pl.BlockSpec((depth, 8 * width), lambda k: (jnp.maximum(k - split, 0), 0)),
        ]
        + [pl.BlockSpec(memory_space=pltpu.HBM)] * len(blocks),
        out_specs=[
            pl.BlockSpec((8, rows, width), lambda k: (0, 0, 0)),
            pl.BlockSpec(memory_space=pltpu.HBM),
        ],
        scratch_shapes=[
            pltpu.VMEM((rows, params), BF16),
            pltpu.VMEM((rows, 8 * width), F32),
            pltpu.SemaphoreType.DMA((len(blocks) + 1,)),
        ],
        compiler_params=pltpu.CompilerParams(vmem_limit_bytes=24 << 20),
        cost_estimate=pl.CostEstimate(
            flops=2 * rows * params * 8 * width, bytes_accessed=16 << 20, transcendentals=0
        ),
    )(first, second, *blocks)


def hash_kernel(part, width, words, gathered, out, examples, total, arrived):
    step = pl.program_id(0)
    steps = arrived.shape[0]
    params = examples.shape[1]
    depth = params // steps
    wide = 512

    def bring(index):
        at = pl.ds(pl.multiple_of(index * depth, depth), depth)
        return pltpu.make_async_copy(gathered.at[:, at], examples.at[:, at], arrived.at[index])

    @pl.when(step == 0)
    def _():
        for index in range(steps):
            bring(index).start()
        total[...] = jnp.zeros_like(total)

    bring(step).wait()
    held = examples[:, pl.ds(pl.multiple_of(step * depth, depth), depth)]
    row_start = first_parameter(step, depth, params)
    for first in range(0, 8 * width, wide):
        made = signs(words, row_start, depth, columns(first, wide, part, width))
        total[:, first : first + wide] += jnp.dot(held, made, preferred_element_type=F32)

    @pl.when(step == steps - 1)
    def _():
        write_run(out, total, width)


def project_hash(part, width, words, gathered, steps=16):
    rows, params = gathered.shape
    return pl.pallas_call(
        functools.partial(hash_kernel, part, width),
        out_shape=jax.ShapeDtypeStruct((8, rows, width), F32),
        grid=(steps,),
        in_specs=[pl.BlockSpec(memory_space=pltpu.SMEM), pl.BlockSpec(memory_space=pltpu.HBM)],
        out_specs=pl.BlockSpec((8, rows, width), lambda k: (0, 0, 0)),
        scratch_shapes=[
            pltpu.VMEM((rows, params), BF16),
            pltpu.VMEM((rows, 8 * width), F32),
            pltpu.SemaphoreType.DMA((steps,)),
        ],
        compiler_params=pltpu.CompilerParams(vmem_limit_bytes=60 << 20),
        cost_estimate=pl.CostEstimate(
            flops=2 * rows * params * 8 * width, bytes_accessed=16 << 20, transcendentals=0
        ),
    )(words, gathered)


def sum_kernel(part, keep, send, whole):
    core = lax.axis_index("c")
    total = part[0]
    for index in range(1, part.shape[0]):
        total += part[index]
    whole[...] = total.astype(BF16)
    for block in range(2):
        for target, which in ((keep, core), (send, 1 - core)):
            start = pl.multiple_of(block * 128 + which * 64, 64)
            target[block * 64 : (block + 1) * 64, :] = whole[pl.ds(start, 64), :]


def sum_parts(part):
    _, rows, width = part.shape
    shapes = [(rows // 2, width), (rows // 2, width)]
    return pl.pallas_call(
        sum_kernel,
        out_shape=[jax.ShapeDtypeStruct(shape, BF16) for shape in shapes],
        scratch_shapes=[pltpu.VMEM((rows, width), BF16)],
        compiler_params=pltpu.CompilerParams(vmem_limit_bytes=8 << 20),
    )(part)


RING = (0, -1, -2, -3, -4, 1, 2, 3)


def condition_kernel(*refs):
    low, high, (mine, other), (out, pieces, tiles, arrived) = refs[0], refs[1:9], refs[9:11], refs[11:]
    core = lax.axis_index("c")
    yl = lax.axis_index("yl")
    z = lax.axis_index("zh") * 2 + lax.axis_index("zl")
    zl = lax.axis_index("zl")
    tile_copies = []
    for group in range(2):
        rows = pl.ds(pl.multiple_of((zl ^ group) * 512, 512), 512)
        for which, (source, place) in enumerate(((mine, core), (other, 1 - core))):
            tile_copies.append(
                pltpu.make_async_copy(
                    source.at[rows, :], tiles.at[place, rows, :], arrived.at[16 + group * 2 + which]
                )
            )
    copies = []
    for index, away in enumerate(RING):
        for run, source in enumerate((low.at[(z + (away + 8)) & 7], high[index])):
            target = pieces.at[index, :, :, run * 128 : (run + 1) * 128]
            copies.append(pltpu.make_async_copy(source, target, arrived.at[index * 2 + run]))
    for group in range(2):
        for copy in tile_copies[group * 2 : group * 2 + 2]:
            copy.start()
        for index, away in enumerate(RING):
            if away % 2 == group:
                copies[index * 2].start()
                copies[index * 2 + 1].start()
    for group in range(2):
        for copy in tile_copies[group * 2 : group * 2 + 2]:
            copy.wait()
        for index, away in enumerate(RING):
            if away % 2 != group:
                continue
            copies[index * 2].wait()
            copies[index * 2 + 1].wait()
            source = (z + (away + 8)) & 7
            total = None
            for flip in range(4):
                start = pl.multiple_of(((zl ^ group) * 2 + (core ^ (flip % 2))) * 256, 256)
                tile = tiles[yl ^ (flip // 2), pl.ds(start, 256), :]
                term = jnp.dot(pieces[index, flip], tile, preferred_element_type=F32)
                total = term if total is None else total + term
            at = pl.ds(pl.multiple_of((source >> 1) * 128, 128), 128)
            if group == 0:
                out[at, :] = total
            else:
                out[at, :] += total


def condition(low, high, mine, other):
    _, flips, rows, width = low.shape
    return pl.pallas_call(
        condition_kernel,
        out_shape=jax.ShapeDtypeStruct((4 * rows, mine.shape[1]), F32),
        in_specs=[pl.BlockSpec(memory_space=pltpu.HBM)] * 11,
        out_specs=pl.BlockSpec(memory_space=pltpu.VMEM),
        scratch_shapes=[
            pltpu.VMEM((8, flips, rows, 2 * width), BF16),
            pltpu.VMEM((2,) + mine.shape, BF16),
            pltpu.SemaphoreType.DMA((20,)),
        ],
        compiler_params=pltpu.CompilerParams(vmem_limit_bytes=60 << 20),
        cost_estimate=pl.CostEstimate(flops=2 * 512 * 2048 * 1024, bytes_accessed=7 << 20, transcendentals=0),
    )(low, *high, mine, other)


def join_kernel(*refs):
    for index, ref in enumerate(refs[:-1]):
        refs[-1][index] = ref[...]


def join(values):
    return pl.pallas_call(
        join_kernel,
        out_shape=jax.ShapeDtypeStruct((len(values),) + values[0].shape, values[0].dtype),
        compiler_params=pltpu.CompilerParams(vmem_limit_bytes=6 << 20),
    )(*values)


def pack_kernel(low, *refs):
    high, (out, arrived) = refs[:8], refs[8:]
    z = lax.axis_index("zh") * 2 + lax.axis_index("zl")
    copies = []
    for index, away in enumerate(RING):
        for run, source in enumerate((low.at[(z + (away + 8)) & 7, 0:2], high[index].at[0:2])):
            copies.append(pltpu.make_async_copy(source, out.at[run, index], arrived.at[index * 2 + run]))
    for copy in copies:
        copy.start()
    for copy in copies:
        copy.wait()


def pack(low, high):
    _, _, rows, width = low.shape
    return pl.pallas_call(
        pack_kernel,
        out_shape=jax.ShapeDtypeStruct((2, 8, 2, rows, width), BF16),
        in_specs=[pl.BlockSpec(memory_space=pltpu.HBM)] * 9,
        out_specs=pl.BlockSpec(memory_space=pltpu.HBM),
        scratch_shapes=[pltpu.SemaphoreType.DMA((16,))],
        compiler_params=pltpu.CompilerParams(vmem_limit_bytes=4 << 20),
    )(low, *high)


def pair_kernel(parts, near, far, out, rows, pairs):
    core = lax.axis_index("c")
    place = lax.axis_index("zh") * 2 + lax.axis_index("zl")
    origin = (lax.axis_index("yh") * 4 + lax.axis_index("x")) ^ place
    total = parts[0]
    for index in range(1, parts.shape[0]):
        total += parts[index]
    rows[...] = total.astype(BF16)
    for half, held in enumerate((near, far)):
        for index, away in enumerate(RING):
            source = (origin + (away + 8)) & 7
            value = None
            for flip in range(2):
                start = ((source & 1) * 2 + (core ^ half ^ flip)) * 256
                term = lax.dot_general(
                    rows[:, pl.ds(pl.multiple_of(start, 256), 256)],
                    jnp.concatenate([held[0, index, flip], held[1, index, flip]], axis=1),
                    (((1,), (1,)), ((), ())),
                    preferred_element_type=F32,
                )
                value = term if value is None else value + term
            pairs[half, source] = value
    for half in range(2):
        for zh in range(4):
            value = pairs[half, zh * 2] + pairs[half, zh * 2 + 1]
            for block in range(2):
                piece = value[:, block * 64 : (block + 1) * 64]
                target = zh * 4 + block * 2 + (core ^ half)
                out[target, :, :64] = piece[:32]
                out[target, :, 64:] = piece[32:]


def pair(parts, near, far):
    return pl.pallas_call(
        pair_kernel,
        out_shape=jax.ShapeDtypeStruct((16, 32, 128), F32),
        scratch_shapes=[pltpu.VMEM((64, 1024), BF16), pltpu.VMEM((2, 8, 64, 128), F32)],
        compiler_params=pltpu.CompilerParams(vmem_limit_bytes=12 << 20),
    )(parts, near, far)


def finish_kernel(parts, out):
    total = parts[0]
    for index in range(1, parts.shape[0]):
        total += parts[index]
    total = total * SCALE
    out[:32] = total[:, :64]
    out[32:] = total[:, 64:]


def finish(parts):
    return pl.pallas_call(finish_kernel, out_shape=jax.ShapeDtypeStruct((64, 64), F32))(parts)


def swap(value, axis):
    return lax.ppermute(value, axis, [(0, 1), (1, 0)])


def step_z(value, by):
    return lax.ppermute(value, ("zh", "zl"), [(i, (i + by) % 8) for i in range(8)])


def ring(value):
    up = [step_z(value, 1)]
    down = [step_z(value, 7)]
    for _ in range(2):
        up.append(step_z(up[-1], 1))
        down.append(step_z(down[-1], 7))
    up.append(step_z(up[-1], 1))
    return [value] + up + down


def flips(keep, send):
    received = swap(send, "c")
    return join([keep, received, swap(keep, "yl"), swap(received, "yl")])


def per_device(gradients, inverse_gram, hash_words):
    half = gradients.shape[0] // 2
    width, depth, params = 128, 1024, 2 * gradients.shape[1]
    split = 5
    first = table(0, width, 0, split, depth, params, hash_words)
    second = table(0, width, split, params // depth - split, depth, params, hash_words)

    next_y = swap(gradients, "yl")
    next_z = swap(gradients, "zl")
    first, next_y, next_z = lax.optimization_barrier((first, next_y, next_z))
    diag_a, diag_b = swap(next_y[:half], "zl"), swap(next_z[half:], "yl")
    diag_a, diag_b, second = lax.optimization_barrier((diag_a, diag_b, second))
    own = [gradients, next_y, next_z, diag_a, diag_b]
    blocks = own + [swap(a, "c") for a in own]
    other_tile = swap(inverse_gram, "c")

    partial, gathered = project_ready(first, second, width, blocks)
    part = lax.all_to_all(partial, CHIPS, 0, 0, tiled=True)
    partial = project_hash(1, width, hash_words, gathered)
    partial, part = lax.optimization_barrier((partial, part))
    next_part = lax.all_to_all(partial, CHIPS, 0, 0, tiled=True)

    keep, send = sum_parts(part)
    mine = flips(keep, send)
    low = lax.all_gather(mine, ("zh", "zl"), axis=0)
    next_part, mine = lax.optimization_barrier((next_part, mine))
    high = ring(flips(*sum_parts(next_part)))

    places = [(z, yl, chip, c) for z in range(8) for yl in range(2) for chip in range(8) for c in range(2)]

    def flat(z, yl, chip, c):
        return ((z * 2 + yl) * 8 + chip) * 2 + c

    across = [(flat(z, yl, chip, c), flat(z, yl, z ^ chip, c)) for z, yl, chip, c in places]
    along = [(flat(z, yl, chip, c), flat(z ^ chip, yl, chip, c)) for z, yl, chip, c in places]
    packed = pack(low, high)
    packed, high = lax.optimization_barrier((packed, high))
    packed = lax.ppermute(packed, EX + PAR, across)
    conditioned = condition(low, high, inverse_gram, other_tile)
    conditioned, packed = lax.optimization_barrier((conditioned, packed))
    near = lax.ppermute(packed, EX + PAR, along)
    parts = lax.all_to_all(conditioned.reshape(8, 64, 1024), CHIPS, 0, 0, tiled=True)
    return finish(lax.all_to_all(pair(parts, near, swap(near, "c")), EX, 0, 0, tiled=True))


def solution(mesh):
    fine = Mesh(mesh.devices.reshape(4, 2, 2, 2, 4, 2), EX + PAR)
    return jax.shard_map(
        per_device,
        mesh=fine,
        in_specs=(P(EX, PAR), P(PAR, EX), P()),
        out_specs=P(PAR, EX),
        check_vma=False,
    )
```
